128 devices in a mesh: gx: 16 (over y, x), gy: 8 (over z, core).
Axes of the slice: x: 4, y: 4, z: 4, core: 2. Of those that a mesh axis runs over, the one named last changes fastest.
Arguments:
- matrix_pressure: float32 [2048, 2048], P('gx', 'gy'), may hold values from 0 to 1
- permeability: float32 [2048, 2048], P('gx', 'gy'), may hold values from 0.2 to 5
- matrix_storage: float32 [2048, 2048], P('gx', 'gy'), may hold values from 0.5 to 2
- fracture_pressure: float32 [512, 128, 128], P(('gx', 'gy')), may hold values from 0 to 0.4
- initial_aperture: float32 [512, 128, 128], P(('gx', 'gy')), may hold values from 0.6 to 2
- normal_stress: float32 [512, 128, 128], P(('gx', 'gy')), may hold values from 0.5 to 4
- isect_cell: int32 [524288], P(('gx', 'gy')), may hold values from 0 to 32767
- isect_owner: int32 [524288, 1], P(('gx', 'gy')), may hold values from 0 to 127; in each aligned block of 4096 rows (0 to 4095, 4096 to 8191, ...) at most 64 rows name the same one
- isect_frac: int32 [524288], P(('gx', 'gy')), may hold values from 0 to 3
- isect_seg: int32 [524288], P(('gx', 'gy')), may hold values from 0 to 16383
- well_index: float32 [524288], P(('gx', 'gy')), may hold values from 0.5 to 5
- junc_frac: int32 [262144], P(('gx', 'gy')), may hold values from 0 to 3
- junc_seg: int32 [262144], P(('gx', 'gy')), may hold values from 0 to 16383
- junc_owner: int32 [262144, 1], P(('gx', 'gy')), may hold values from 0 to 127; in each aligned block of 2048 rows (0 to 2047, 2048 to 4095, ...) at most 32 rows name the same one
- junc_far_frac: int32 [262144], P(('gx', 'gy')), may hold values from 0 to 3
- junc_far_seg: int32 [262144], P(('gx', 'gy')), may hold values from 0 to 16383
- junc_trans: float32 [262144], P(('gx', 'gy')), may hold values from 0.5 to 5
Outputs:
- fracture_new: float32 [512, 128, 128], P(('gx', 'gy'))
- matrix_new: float32 [2048, 2048], P('gx', 'gy')
The draws below stay inside these ranges and needn't reach their ends.
Inputs may be any that keep to these rules, and one draw needn't show every extreme that they name: `isect_owner`: in the rows of one device no owner is named by more than 64 rows, and some owner reaches 64. `junc_owner`: in the rows of one device no owner is named by more than 32 rows, and some owner reaches 32.
All inputs are finite; a program needn't handle non-finite values.
Results may differ from the reference program's by a relative error of at most 0.0003.
Values sent between devices are 32-bit elements; how exact they have to be, the bound alone decides.
A program may use at most 64 MiB of HBM per device.

```python
import math
import jax
import jax.numpy as jnp
import numpy as np

CX = 128
CY = 256
FR_DEV = 4
FS = 128
ISECT_DEV = 4096
JN_DEV = 2048
SWEEPS = 3
CAP = 64
CAPJ = 32
NX = 2048
NY = 2048
FRACS = 512
ISECTS = 524288
JUNCS = 262144
N_GY = 8
DEVICES = 128


def set_ends(values, rng, low, top_value):
    place = [jax.random.randint(jax.random.fold_in(rng, axis), (), 0, length) for axis, length in enumerate(values.shape)]
    main_axis = values.shape.index(max(values.shape))
    beside = place[:main_axis] + [(place[main_axis] + 1) % values.shape[main_axis]] + place[main_axis + 1:]
    return values.at[tuple(place)].set(low).at[tuple(beside)].set(top_value)


def block_scale(rng, dims, pieces, low, high):
    gain, own = 1.0, jax.random.fold_in(rng, 6)
    for dim, shards_of in pieces:
        draws = jnp.exp(jax.random.uniform(jax.random.fold_in(own, dim), (shards_of,), jnp.float32, low / len(pieces), high / len(pieces)))
        gain = gain * jnp.repeat(draws, dims[dim] // shards_of).reshape([-1 if axis == dim else 1 for axis in range(len(dims))])
    return gain


def shared_out(own_key, own, number, rows, count, top, most, skew):
    ranking = jax.random.permutation(own_key, count)
    crowded, usual = shares(count, rows * top, most, skew, True), shares(count, rows * top, most, skew, False)
    places = jnp.arange(count)

    def named(tallies, rotation):
        used = int((tallies > 0).sum())
        fixed = max(1, used // 4)
        shifted = fixed + (places - fixed + rotation * (used - fixed)) % max(1, count - fixed)
        return jnp.zeros((count,), jnp.int32).at[ranking[jnp.where(places < fixed, places, shifted)]].set(jnp.asarray(tallies, jnp.int32))

    tallies = jnp.where(number % 4 == 0, named(crowded, number // 4), named(usual, number - number // 4 - 1))
    mixed = jax.random.permutation(jax.random.fold_in(own, 3), count)
    donor, sink = mixed[0:count // 2 * 2:2], mixed[1:count // 2 * 2:2]
    slack = jnp.minimum(tallies[donor] - 1, most - tallies[sink]) // 2
    slack = jnp.where((donor == ranking[0]) | (sink == ranking[0]) | (tallies[sink] == 0), 0, jnp.maximum(slack, 0))
    shifted = jax.random.randint(jax.random.fold_in(own, 4), (count // 2,), 0, 1 << 20) % (slack + 1)
    tallies = tallies.at[donor].add(-shifted).at[sink].add(shifted)
    items = jnp.searchsorted(jnp.cumsum(tallies), jnp.arange(rows * top), side="right").astype(jnp.int32)
    table = items.reshape(top, rows).T
    table = table[jax.random.permutation(jax.random.fold_in(own, 1), rows)]
    rotation = jax.random.randint(jax.random.fold_in(own, 2), (rows, 1), 0, top)
    return jnp.take_along_axis(table, (jnp.arange(top)[None, :] + rotation) % top, axis=1)


def shares(count, total, reach, slope, full):
    loads = [(1 << 20) // math.isqrt(rank ** slope) + 1 for rank in range(1, count + 1)]
    largest = reach if full else min(reach, max(-(-total // count), total * loads[0] // sum(loads)))
    least = 1 if total - largest >= count - 1 else 0
    holding, spare = [largest] + [least] * (count - 1), total - largest - least * (count - 1)
    while spare > 0:
        free = [i for i in range(1, count) if holding[i] < largest] or [i for i in range(1, count) if holding[i] < reach]
        whole, left = sum([loads[i] for i in free]), spare
        for i in free:
            extra = min(reach - holding[i], max(1, left * loads[i] // whole), spare)
            holding[i] = holding[i] + extra
            spare = spare - extra
    return np.array(holding)


def setup_inputs(seed: int = 0) -> dict:
    seeds = jax.random.split(jax.random.key(seed), 18)
    matrix_pressure = jnp.clip(1.0 * jax.random.uniform(seeds[0], (NX, NY), jnp.float32) ** block_scale(seeds[0], (NX, NY), ((0, 16), (1, 8)), -0.2, 0.2), 0.0, 1.0)
    permeability = jnp.clip(jnp.exp(math.log(5.0) - 3.218876 * jax.random.uniform(seeds[1], (NX, NY), jnp.float32) ** block_scale(seeds[1], (NX, NY), ((0, 16), (1, 8)), -0.2, 0.2)), 0.2, 5.0)
    matrix_storage = jnp.clip(jnp.exp(math.log(2.0) - 1.3862944 * jax.random.uniform(seeds[2], (NX, NY), jnp.float32) ** block_scale(seeds[2], (NX, NY), ((0, 16), (1, 8)), -0.2, 0.2)), 0.5, 2.0)
    fracture_pressure = jnp.clip(0.4 * jax.random.uniform(seeds[3], (FRACS, FS, FS), jnp.float32) ** block_scale(seeds[3], (FRACS, FS, FS), ((0, 128),), -0.2, 0.2), 0.0, 0.4)
    initial_aperture = jnp.clip(jnp.exp(math.log(2.0) - 1.2039728 * jax.random.uniform(seeds[4], (FRACS, FS, FS), jnp.float32) ** block_scale(seeds[4], (FRACS, FS, FS), ((0, 128),), -0.2, 0.2)), 0.6, 2.0)
    normal_stress = jnp.clip(0.5 + 3.5 * jax.random.uniform(seeds[5], (FRACS, FS, FS), jnp.float32) ** block_scale(seeds[5], (FRACS, FS, FS), ((0, 128),), -0.2, 0.2), 0.5, 4.0)
    isect_cell = set_ends(jax.random.randint(seeds[6], (ISECTS,), 0, CX * CY), jax.random.fold_in(seeds[6], 1), 0, (CX * CY) - 1).astype(jnp.int32)
    isect_owner_keys = jax.random.split(jax.random.fold_in(seeds[7], 1), ISECTS // ISECT_DEV)
    isect_owner_turns = jax.random.permutation(jax.random.fold_in(seeds[7], 3), ISECTS // ISECT_DEV)
    isect_owner = jax.vmap(lambda own, number: shared_out(jax.random.fold_in(seeds[7], 2), own, number, ISECT_DEV, DEVICES, 1, CAP, 2))(isect_owner_keys, isect_owner_turns).reshape((ISECTS, 1))
    isect_frac = set_ends(jax.random.randint(seeds[8], (ISECTS,), 0, FR_DEV), jax.random.fold_in(seeds[8], 1), 0, FR_DEV - 1).astype(jnp.int32)
    isect_seg = set_ends(jax.random.randint(seeds[9], (ISECTS,), 0, FS * FS), jax.random.fold_in(seeds[9], 1), 0, (FS * FS) - 1).astype(jnp.int32)
    well_index = jnp.clip(jnp.exp(math.log(5.0) - 2.3025851 * jax.random.uniform(seeds[10], (ISECTS,), jnp.float32) ** block_scale(seeds[10], (ISECTS,), ((0, 128),), -0.2, 0.2)), 0.5, 5.0)
    junc_frac = set_ends(jax.random.randint(seeds[11], (JUNCS,), 0, FR_DEV), jax.random.fold_in(seeds[11], 1), 0, FR_DEV - 1).astype(jnp.int32)
    junc_seg = set_ends(jax.random.randint(seeds[12], (JUNCS,), 0, FS * FS), jax.random.fold_in(seeds[12], 1), 0, (FS * FS) - 1).astype(jnp.int32)
    junc_owner_keys = jax.random.split(jax.random.fold_in(seeds[13], 1), JUNCS // JN_DEV)
    junc_owner_turns = jax.random.permutation(jax.random.fold_in(seeds[13], 3), JUNCS // JN_DEV)
    junc_owner = jax.vmap(lambda own, number: shared_out(jax.random.fold_in(seeds[13], 2), own, number, JN_DEV, DEVICES, 1, CAPJ, 1))(junc_owner_keys, junc_owner_turns).reshape((JUNCS, 1))
    junc_far_frac = set_ends(jax.random.randint(seeds[14], (JUNCS,), 0, FR_DEV), jax.random.fold_in(seeds[14], 1), 0, FR_DEV - 1).astype(jnp.int32)
    junc_far_seg = set_ends(jax.random.randint(seeds[15], (JUNCS,), 0, FS * FS), jax.random.fold_in(seeds[15], 1), 0, (FS * FS) - 1).astype(jnp.int32)
    junc_trans = jnp.clip(jnp.exp(math.log(5.0) - 2.3025851 * jax.random.uniform(seeds[16], (JUNCS,), jnp.float32) ** block_scale(seeds[16], (JUNCS,), ((0, 128),), -0.2, 0.2)), 0.5, 5.0)
    return {"matrix_pressure": matrix_pressure, "permeability": permeability, "matrix_storage": matrix_storage, "fracture_pressure": fracture_pressure, "initial_aperture": initial_aperture, "normal_stress": normal_stress, "isect_cell": isect_cell, "isect_owner": isect_owner, "isect_frac": isect_frac, "isect_seg": isect_seg, "well_index": well_index, "junc_frac": junc_frac, "junc_seg": junc_seg, "junc_owner": junc_owner, "junc_far_frac": junc_far_frac, "junc_far_seg": junc_far_seg, "junc_trans": junc_trans}


def harmonic(first, second):
    return 2.0 * first * second / (first + second)


def reference(matrix_pressure, permeability, matrix_storage, fracture_pressure, initial_aperture, normal_stress, isect_cell, isect_owner, isect_frac, isect_seg, well_index, junc_frac, junc_seg, junc_owner, junc_far_frac, junc_far_seg, junc_trans):
    area = FS * FS
    effective = normal_stress - fracture_pressure
    aperture = initial_aperture - 0.5 * effective / (0.5 + effective)
    conduct = aperture * aperture * aperture
    face_rows = harmonic(conduct[:, 1:, :], conduct[:, :-1, :])
    face_cols = harmonic(conduct[:, :, 1:], conduct[:, :, :-1])
    north = jnp.pad(face_rows, ((0, 0), (1, 0), (0, 0)))
    south = jnp.pad(face_rows, ((0, 0), (0, 1), (0, 0)))
    west = jnp.pad(face_cols, ((0, 0), (0, 0), (1, 0)))
    east = jnp.pad(face_cols, ((0, 0), (0, 0), (0, 1)))
    device = (jnp.arange(ISECTS, dtype=jnp.int32) // ISECT_DEV).astype(jnp.int32)
    grid_row = (device // N_GY) * CX + isect_cell // CY
    grid_col = (device % N_GY) * CY + isect_cell % CY
    matrix_flat = (grid_row * NY + grid_col).astype(jnp.int32)
    frac_flat = ((isect_owner[:, 0] * FR_DEV + isect_frac) * area + isect_seg).astype(jnp.int32)
    sampled = matrix_pressure.reshape(-1)[matrix_flat]
    source_diag = jnp.zeros((FRACS * area,), jnp.float32).at[frac_flat].add(well_index)
    source_rhs = jnp.zeros((FRACS * area,), jnp.float32).at[frac_flat].add(well_index * sampled)
    jdevice = (jnp.arange(JUNCS, dtype=jnp.int32) // JN_DEV).astype(jnp.int32)
    near_flat = ((jdevice * FR_DEV + junc_frac) * area + junc_seg).astype(jnp.int32)
    far_flat = ((junc_owner[:, 0] * FR_DEV + junc_far_frac) * area + junc_far_seg).astype(jnp.int32)
    junc_diag = jnp.zeros((FRACS * area,), jnp.float32).at[near_flat].add(junc_trans)
    shape = fracture_pressure.shape
    denom = aperture + north + south + west + east + source_diag.reshape(shape) + junc_diag.reshape(shape)
    stored = aperture * fracture_pressure + source_rhs.reshape(shape)
    current = fracture_pressure
    for sweep in range(SWEEPS):
        padded = jnp.pad(current, ((0, 0), (1, 1), (1, 1)))
        partner = current.reshape(-1)[far_flat]
        junc_rhs = jnp.zeros((FRACS * area,), jnp.float32).at[near_flat].add(junc_trans * partner)
        total = stored + north * padded[:, :-2, 1:-1] + south * padded[:, 2:, 1:-1]
        total = total + west * padded[:, 1:-1, :-2] + east * padded[:, 1:-1, 2:] + junc_rhs.reshape(shape)
        current = total / denom
    fracture_new = current
    at_fracture = fracture_new.reshape(-1)[frac_flat]
    m_diag = jnp.zeros((NX * NY,), jnp.float32).at[matrix_flat].add(well_index).reshape(NX, NY)
    m_rhs = jnp.zeros((NX * NY,), jnp.float32).at[matrix_flat].add(well_index * at_fracture).reshape(NX, NY)
    press = jnp.pad(matrix_pressure, 1)
    perm = jnp.pad(permeability, 1)
    total = matrix_storage * matrix_pressure + m_rhs
    weights = matrix_storage + m_diag
    for (a, b) in ((0, 1), (2, 1), (1, 0), (1, 2)):
        face = harmonic(permeability, perm[a:a + NX, b:b + NY])
        total = total + face * press[a:a + NX, b:b + NY]
        weights = weights + face
    matrix_new = total / weights
    return fracture_new, matrix_new
```

```python
import jax
import jax.numpy as jnp
from jax import lax
from jax.experimental import pallas as pl
from jax.experimental.pallas import tpu as pltpu
from jax.sharding import PartitionSpec as P

LOGICAL = pl.DeviceIdType.LOGICAL
F32 = jnp.float32
BF16 = jnp.bfloat16
SWEEPS = 3
D = 128
QJ = 32
QI = 64


def dot_nn(a, b):
    return lax.dot_general(a, b, (((1,), (0,)), ((), ())), preferred_element_type=F32)


def dot_nt(a, b):
    return lax.dot_general(a, b, (((1,), (1,)), ((), ())), preferred_element_type=F32)


def halves(x):
    high = x.astype(BF16).astype(F32)
    return high, (x - high).astype(BF16).astype(F32)


def spread(row, rows):
    n = row.shape[1]
    block = jnp.broadcast_to(row, (16, n)).astype(BF16)
    return jnp.broadcast_to(block[None], (rows // 16, 16, n))


def counter(rows, n):
    return (
        (lax.broadcasted_iota(jnp.int32, (rows // 16, 16, n), 0) * 16
         + lax.broadcasted_iota(jnp.int32, (rows // 16, 16, n), 1)).astype(F32).astype(BF16)
    )


def hot(row, rows):
    n = row.shape[1]
    mask = counter(rows, n) == spread(row, rows)
    return jnp.where(mask, BF16(1), BF16(0)).reshape(rows, n)


def hot_values(row, values, rows):
    n = row.shape[1]
    mask = counter(rows, n) == spread(row, rows)
    return [
        jnp.where(mask, spread(v, rows), jnp.zeros((rows // 16, 16, n), BF16)).reshape(rows, n)
        for v in values
    ]


def hot512(row):
    return hot(row, 256), hot(row - 256.0, 256)


def divide(x, by):
    whole = jnp.floor(x * (1.0 / by))
    return whole, x - whole * by


def harmonic(first, second):
    return 2.0 * first * second / (first + second)


def kernel(
    mp, perm, stor, fp, ia, ns,
    icell, iown, ifrac, iseg, wi,
    jfrac, jseg, jown, jffrac, jfseg, jtrans,
    fnew, mnew,
    hot_own, hot_slot, col_hot, own_slot, own_q,
    tri, base,
    near_r, near_j, near_t, served_r, served_j, isr_r, isr_j, isr_w, isr_ws, cell_r, cell_c, cell_w,
    work, rhot_srv, rhot_near, rhot_is, rhot_cells, lv, tbl,
    q_now, cn, cs, cw, ce, inv, sto, apt, m_tot, m_wts,
    jsend, jrecv, isend, irecv, asend, arecv, rsend, rrecv, hsend, hrecv,
    send_sem, recv_sem, hsend_sem, hrecv_sem,
):
    gx = lax.axis_index("gx")
    gy = lax.axis_index("gy")
    me = gx * 8 + gy
    bar = pltpu.get_barrier_semaphore()

    def greet(k, c):
        pl.semaphore_signal(bar, inc=1, device_id=lax.rem(me + k, D), device_id_type=LOGICAL)
        return c

    lax.fori_loop(1, D, greet, 0)

    def exchange(number, src, dst, rows):
        def send(k, c):
            t = lax.rem(me + (D // 2) + k, D)
            pltpu.make_async_remote_copy(
                src.at[lax.rem(t, rows)], dst.at[me], send_sem.at[number], recv_sem.at[number],
                device_id=t, device_id_type=LOGICAL,
            ).start()
            return c

        lax.fori_loop(0, D // 2, send, 0)
        lax.fori_loop(D // 2 + 1, D, send, 0)
        pltpu.make_async_copy(src.at[lax.rem(me, rows)], dst.at[me], recv_sem.at[number]).start()

    def arrived(number, dst):
        pltpu.make_async_copy(dst, dst, recv_sem.at[number]).wait()

    def sent(number, dst):
        part = dst.at[pl.ds(0, D - 1)]
        pltpu.make_async_copy(part, part, send_sem.at[number]).wait()

    def merge(got, rows):
        blocks = D // rows
        width = D // blocks
        mine = me // rows
        lane_block = lax.broadcasted_iota(jnp.int32, (rows, D), 1) // width
        out = jnp.zeros((rows, D), F32)
        for k in range(blocks):
            part = pltpu.roll(got[k * rows:(k + 1) * rows, :], lax.rem((k - mine + blocks) * width, D), 1)
            out = jnp.where(lane_block == k, part, out)
        return out

    tri[...] = jnp.where(
        lax.broadcasted_iota(jnp.int32, (256, 256), 0) <= lax.broadcasted_iota(jnp.int32, (256, 256), 1), 1.0, 0.0
    ).astype(BF16)

    def slots(own_ref, count, rows, q_out, lane_out):
        width = rows
        base[...] = jnp.zeros((D, D), F32)

        def chunk(c, carry):
            for h in range(2):
                own = own_ref[pl.ds(2 * c + h, 1), :]
                mask = lax.broadcasted_iota(jnp.int32, (D, D), 0) == own
                hot_own[:, h * D:(h + 1) * D] = jnp.where(mask, 1.0, 0.0).astype(BF16)
            upto = dot_nn(hot_own[...], tri[...])
            before = base[...]
            for h in range(2):
                own = own_ref[pl.ds(2 * c + h, 1), :]
                mask = lax.broadcasted_iota(jnp.int32, (D, D), 0) == own
                rank = jnp.sum(jnp.where(mask, upto[:, h * D:(h + 1) * D] + before, 0.0), axis=0, keepdims=True) - 1.0
                block, rest = divide(own.astype(F32), rows)
                q_out[pl.ds(2 * c + h, 1), :] = rest
                lane_out[pl.ds(2 * c + h, 1), :] = block * width + rank
            base[...] = before + jnp.broadcast_to(upto[:, 255:256], (D, D))
            return carry

        lax.fori_loop(0, count // 2, chunk, 0)

    def pack(count, rows, values_of, planes):
        def chunk(c, carry):
            q = own_q[pl.ds(c, 1), :]
            at = pl.ds(pl.multiple_of(c * D, D), D)
            hot_slot[0:rows, at] = hot(q, rows)
            for p, v in enumerate(hot_values(own_slot[pl.ds(c, 1), :], values_of(c), D)):
                lv[p * D:(p + 1) * D, at] = v
            return carry

        lax.fori_loop(0, count, chunk, 0)
        out = dot_nt(hot_slot[0:rows, 0:count * D], lv[0:planes * D, 0:count * D])
        return [out[:, p * D:(p + 1) * D] for p in range(planes)]

    def gather(table, hots, j_ref, chunks, out):
        def chunk(c, carry):
            at = pl.ds(pl.multiple_of(c * 256, 256), 256)
            got = dot_nn(table[...], hots[:, at])
            both = got[0:D, :] + got[D:2 * D, :]
            for h in range(2):
                mask = lax.broadcasted_iota(jnp.int32, (D, D), 0) == j_ref[pl.ds(2 * c + h, 1), :].astype(jnp.int32)
                row = jnp.sum(jnp.where(mask, both[:, h * D:(h + 1) * D], 0.0), axis=0, keepdims=True)
                out(2 * c + h, row)
            return carry

        lax.fori_loop(0, chunks // 2, chunk, 0)

    def scatter(values, hots, j_ref, chunks):
        parts = 2 * len(values)

        def chunk(c, carry):
            at = pl.ds(pl.multiple_of(c * D, D), D)
            rows = []
            for v in values:
                rows.extend(halves(v[pl.ds(c, 1), :]))
            for p, v in enumerate(hot_values(j_ref[pl.ds(c, 1), :], rows, D)):
                lv[p * D:(p + 1) * D, at] = v
            return carry

        lax.fori_loop(0, chunks, chunk, 0)
        out = []
        for p in range(len(values)):
            both = dot_nt(lv[2 * p * D:(2 * p + 2) * D, 0:chunks * D], hots[...])
            out.append(both[0:D, :] + both[D:2 * D, :])
        return out

    def build512(r_ref, hots, chunks):
        def chunk(c, carry):
            at = pl.ds(pl.multiple_of(c * D, D), D)
            low, high = hot512(r_ref[pl.ds(c, 1), :])
            hots[0:256, at] = low
            hots[256:512, at] = high
            return carry

        lax.fori_loop(0, chunks, chunk, 0)

    def set_table(q):
        high, low = halves(q)
        tbl[0:D, :] = high.astype(BF16)
        tbl[D:2 * D, :] = low.astype(BF16)

    slots(jown, 16, QJ, own_q, own_slot)

    def requests(c):
        high, low = divide((jffrac[pl.ds(c, 1), :] * (D * D) + jfseg[pl.ds(c, 1), :]).astype(F32), 256)
        nigh, nlow = divide((jfrac[pl.ds(c, 1), :] * (D * D) + jseg[pl.ds(c, 1), :]).astype(F32), 256)
        t_high, t_low = halves(jtrans[pl.ds(c, 1), :])
        return [high * 256.0, low, nigh * 256.0, nlow, t_high, t_low]

    r_high, r_low, n_high, n_low, t_high, t_low = pack(16, QJ, requests, 6)
    jsend[:, 0, :] = r_high + r_low
    row, col = divide(n_high + n_low, D)
    near_r[...] = row
    near_j[...] = col
    near_t[...] = t_high + t_low
    pl.semaphore_wait(bar, D - 1)
    exchange(0, jsend, jrecv, QJ)

    p_high, p_low = halves(mp[...])
    work[0:D, :] = p_high.astype(BF16)
    work[D:2 * D, :] = p_low.astype(BF16)

    def cell_hots(c, carry):
        unused, col = divide(icell[pl.ds(c, 1), :].astype(F32), 256)
        col_hot[:, pl.ds(pl.multiple_of(c * D, D), D)] = hot(col, 256)
        cell_r[pl.ds(c, 1), :] = unused
        return carry

    lax.fori_loop(0, 32, cell_hots, 0)

    def keep_sample(c, row):
        isr_ws[pl.ds(c, 1), :] = row * wi[pl.ds(c, 1), :]

    gather(work, col_hot, cell_r, 32, keep_sample)
    slots(iown, 32, QI, own_q, own_slot)

    def wells(c):
        high, low = divide((ifrac[pl.ds(c, 1), :] * (D * D) + iseg[pl.ds(c, 1), :]).astype(F32), 256)
        c_high, c_low = divide(icell[pl.ds(c, 1), :].astype(F32), 256)
        w_high, w_low = halves(wi[pl.ds(c, 1), :])
        s_high, s_low = halves(isr_ws[pl.ds(c, 1), :])
        return [high * 256.0, low, w_high, w_low, s_high, s_low, c_high, c_low]

    i_high, i_low, w_high, w_low, s_high, s_low, c_high, c_low = pack(32, QI, wells, 8)
    isend[:, 0, 0, :] = i_high + i_low
    isend[:, 1, 0, :] = w_high + w_low
    isend[:, 2, 0, :] = s_high + s_low
    exchange(1, isend, irecv, QI)
    cell_r[...] = c_high
    cell_c[...] = c_low
    cell_w[...] = w_high + w_low

    for f in range(4):
        at = slice(f * D, (f + 1) * D)
        p0 = fp[f].T
        effective = ns[f].T - p0
        q_now[:, at] = p0
        apt[:, at] = ia[f].T - 0.5 * effective / (0.5 + effective)
    set_table(q_now[...])

    def answer(round_number):
        def keep(c, row):
            asend[round_number, pl.ds(c, 1), 0, :] = row

        gather(tbl, rhot_srv, served_j, QJ, keep)
        exchange(2 + round_number, asend.at[round_number], arecv.at[round_number], QJ)

    arrived(0, jrecv)
    row, col = divide(merge(jrecv[:, 0, :], QJ), D)
    served_r[...] = row
    served_j[...] = col
    build512(served_r, rhot_srv, QJ)
    answer(0)

    build512(near_r, rhot_near, QJ)
    (junc_diag,) = scatter([near_t], rhot_near, near_j, QJ)
    inv[...] = junc_diag
    arrived(1, irecv)
    row, col = divide(merge(irecv[:, 0, 0, :], QI), D)
    isr_r[...] = row
    isr_j[...] = col
    isr_w[...] = merge(irecv[:, 1, 0, :], QI)
    isr_ws[...] = merge(irecv[:, 2, 0, :], QI)
    build512(isr_r, rhot_is, QI)
    diag, rhs = scatter([isr_w, isr_ws], rhot_is, isr_j, QI)
    inv[...] += diag
    sto[...] = rhs
    lane = lax.broadcasted_iota(jnp.int32, (D, D), 1)
    sub = lax.broadcasted_iota(jnp.int32, (D, D), 0)
    for f in range(4):
        at = slice(f * D, (f + 1) * D)
        ap = apt[:, at]
        cond = ap * ap * ap
        north = jnp.where(lane == 0, 0.0, harmonic(cond, pltpu.roll(cond, 1, 1)))
        south = jnp.where(lane == D - 1, 0.0, harmonic(cond, pltpu.roll(cond, D - 1, 1)))
        west = jnp.where(sub == 0, 0.0, harmonic(cond, pltpu.roll(cond, 1, 0)))
        east = jnp.where(sub == D - 1, 0.0, harmonic(cond, pltpu.roll(cond, D - 1, 0)))
        one = 1.0 / (ap + north + south + west + east + inv[:, at])
        inv[:, at] = one
        cn[:, at] = north * one
        cs[:, at] = south * one
        cw[:, at] = west * one
        ce[:, at] = east * one
        sto[:, at] = (ap * q_now[:, at] + sto[:, at]) * one

    def sweep(round_number):
        arrived(2 + round_number, arecv.at[round_number])
        served_r[...] = merge(arecv[round_number, :, 0, :], QJ) * near_t[...]
        (joined,) = scatter([served_r], rhot_near, near_j, QJ)
        for f in range(4):
            at = slice(f * D, (f + 1) * D)
            q = q_now[:, at]
            q_now[:, at] = (
                sto[:, at]
                + cn[:, at] * pltpu.roll(q, 1, 1)
                + cs[:, at] * pltpu.roll(q, D - 1, 1)
                + cw[:, at] * pltpu.roll(q, 1, 0)
                + ce[:, at] * pltpu.roll(q, D - 1, 0)
                + inv[:, at] * joined[:, at]
            )
        set_table(q_now[...])

    sweep(0)
    answer(1)

    hsend[0, 0, 0, :] = mp[0, 0:D]
    hsend[0, 1, 0, :] = mp[0, D:2 * D]
    hsend[0, 2, 0, :] = perm[0, 0:D]
    hsend[0, 3, 0, :] = perm[0, D:2 * D]
    hsend[1, 0, 0, :] = mp[D - 1, 0:D]
    hsend[1, 1, 0, :] = mp[D - 1, D:2 * D]
    hsend[1, 2, 0, :] = perm[D - 1, 0:D]
    hsend[1, 3, 0, :] = perm[D - 1, D:2 * D]
    mp_left = mp[:, 0:D].T
    mp_right = mp[:, D:2 * D].T
    perm_left = perm[:, 0:D].T
    perm_right = perm[:, D:2 * D].T
    hsend[2, 0, 0, :] = mp_left[0, :]
    hsend[2, 2, 0, :] = perm_left[0, :]
    hsend[3, 0, 0, :] = mp_right[D - 1, :]
    hsend[3, 2, 0, :] = perm_right[D - 1, :]
    hsend[2, 1, 0, :] = mp_left[0, :]
    hsend[2, 3, 0, :] = perm_left[0, :]
    hsend[3, 1, 0, :] = mp_right[D - 1, :]
    hsend[3, 3, 0, :] = perm_right[D - 1, :]
    targets = (
        lax.rem(gx + 15, 16) * 8 + gy,
        lax.rem(gx + 1, 16) * 8 + gy,
        gx * 8 + lax.rem(gy + 7, 8),
        gx * 8 + lax.rem(gy + 1, 8),
    )
    halo = [
        pltpu.make_async_remote_copy(
            hsend.at[n], hrecv.at[n], hsend_sem.at[n], hrecv_sem.at[n], device_id=t, device_id_type=LOGICAL
        )
        for n, t in enumerate(targets)
    ]
    for copy in halo:
        copy.start()
    def cell_slots(c, carry):
        at = pl.ds(pl.multiple_of(c * D, D), D)
        rhot_cells[:, at] = hot(cell_c[pl.ds(c, 1), :], 256)
        return carry

    lax.fori_loop(0, QI, cell_slots, 0)
    (m_diag,) = scatter([cell_w], rhot_cells, cell_r, QI)
    m_wts[...] = stor[...] + m_diag

    sweep(1)
    answer(2)

    for copy in halo:
        copy.wait()
    press, k = mp[...], perm[...]
    rows = lax.broadcasted_iota(jnp.int32, (D, 256), 0)
    cols = lax.broadcasted_iota(jnp.int32, (D, 256), 1)

    def wide(n, plane):
        return jnp.concatenate([hrecv[n, plane], hrecv[n, plane + 1]], axis=1)

    def tall(n, plane):
        column = jnp.broadcast_to(hrecv[n, plane], (D, D)).T
        return jnp.concatenate([column, column], axis=1)

    total = stor[...] * press
    weights = m_wts[...]
    for n, shift, axis, at_edge, outside in (
        (1, 1, 0, rows == 0, gx == 0),
        (0, D - 1, 0, rows == D - 1, gx == 15),
        (3, 1, 1, cols == 0, gy == 0),
        (2, 255, 1, cols == 255, gy == 7),
    ):
        far_p = wide(n, 0) if axis == 0 else tall(n, 0)
        far_k = wide(n, 2) if axis == 0 else tall(n, 2)
        beside_p = jnp.where(at_edge, far_p, pltpu.roll(press, shift, axis))
        beside_k = jnp.where(at_edge, far_k, pltpu.roll(k, shift, axis))
        gone = jnp.where(outside, 0.0, 1.0)
        face = harmonic(k, beside_k) * jnp.where(at_edge, gone, 1.0)
        total = total + face * beside_p
        weights = weights + face
    m_tot[...] = total
    m_wts[...] = weights

    sweep(2)

    def keep_reply(c, row):
        rsend[pl.ds(c, 1), 0, :] = row

    gather(tbl, rhot_is, isr_j, QI, keep_reply)
    exchange(5, rsend, rrecv, QI)
    for f in range(4):
        fnew[f] = q_now[:, f * D:(f + 1) * D].T
    arrived(5, rrecv)
    isr_ws[...] = merge(rrecv[:, 0, :], QI) * cell_w[...]
    (m_rhs,) = scatter([isr_ws], rhot_cells, cell_r, QI)
    mnew[...] = (m_tot[...] + m_rhs) / m_wts[...]

    sent(0, jrecv)
    sent(1, irecv)
    for n in range(SWEEPS):
        sent(2 + n, arecv.at[n])
    sent(5, rrecv)


def shards(
    matrix_pressure, permeability, matrix_storage, fracture_pressure, initial_aperture, normal_stress,
    isect_cell, isect_owner, isect_frac, isect_seg, well_index,
    junc_frac, junc_seg, junc_owner, junc_far_frac, junc_far_seg, junc_trans,
):
    lanes = [
        a.reshape(-1, D)
        for a in (
            isect_cell, isect_owner, isect_frac, isect_seg, well_index,
            junc_frac, junc_seg, junc_owner, junc_far_frac, junc_far_seg, junc_trans,
        )
    ]
    vm = pltpu.VMEM
    scratch = [
        vm((D, 256), BF16),
        vm((QI, 4096), BF16),
        vm((256, 4096), BF16),
        vm((QI, D), F32),
        vm((QI, D), F32),
        vm((256, 256), BF16),
        vm((D, D), F32),
    ]
    scratch += [vm((QJ, D), F32)] * 5
    scratch += [vm((QI, D), F32)] * 7
    scratch += [
        vm((256, 256), BF16),
        vm((512, 4096), BF16),
        vm((512, 4096), BF16),
        vm((512, 8192), BF16),
        vm((256, 8192), BF16),
        vm((1024, 8192), BF16),
        vm((256, 512), BF16),
    ]
    scratch += [vm((D, 512), F32)] * 8
    scratch += [vm((D, 256), F32)] * 2
    scratch += [
        vm((QJ, 1, D), F32),
        vm((D, 1, D), F32),
        vm((QI, 3, 1, D), F32),
        vm((D, 3, 1, D), F32),
        vm((SWEEPS, QJ, 1, D), F32),
        vm((SWEEPS, D, 1, D), F32),
        vm((QI, 1, D), F32),
        vm((D, 1, D), F32),
        vm((4, 4, 1, D), F32),
        vm((4, 4, 1, D), F32),
        pltpu.SemaphoreType.DMA((6,)),
        pltpu.SemaphoreType.DMA((6,)),
        pltpu.SemaphoreType.DMA((4,)),
        pltpu.SemaphoreType.DMA((4,)),
    ]
    return pl.pallas_call(
        kernel,
        out_shape=(
            jax.ShapeDtypeStruct(fracture_pressure.shape, F32),
            jax.ShapeDtypeStruct(matrix_pressure.shape, F32),
        ),
        in_specs=[pl.BlockSpec(memory_space=pltpu.VMEM)] * 17,
        out_specs=(pl.BlockSpec(memory_space=pltpu.VMEM),) * 2,
        scratch_shapes=scratch,
        compiler_params=pltpu.CompilerParams(
            collective_id=0, has_side_effects=True, vmem_limit_bytes=60 << 20
        ),
    )(matrix_pressure, permeability, matrix_storage, fracture_pressure, initial_aperture, normal_stress, *lanes)


def solution(mesh):
    in_specs = (
        (P("gx", "gy"),) * 3
        + (P(("gx", "gy"), None, None),) * 3
        + (P(("gx", "gy")), P(("gx", "gy"), None), P(("gx", "gy")), P(("gx", "gy")), P(("gx", "gy")))
        + (P(("gx", "gy")), P(("gx", "gy")), P(("gx", "gy"), None), P(("gx", "gy")), P(("gx", "gy")), P(("gx", "gy")))
    )
    out_specs = (P(("gx", "gy"), None, None), P("gx", "gy"))
    return jax.shard_map(shards, mesh=mesh, in_specs=in_specs, out_specs=out_specs, check_vma=False)
```

```python
import jax
import jax.numpy as jnp
from jax import lax
from jax.experimental import pallas as pl
from jax.experimental.pallas import tpu as pltpu
from jax.sharding import PartitionSpec as P

LOGICAL = pl.DeviceIdType.LOGICAL
F32 = jnp.float32
BF16 = jnp.bfloat16
SWEEPS = 3
D = 128
QJ = 32
QI = 64


def dot_nn(a, b):
    return lax.dot_general(a, b, (((1,), (0,)), ((), ())), preferred_element_type=F32)


def dot_nt(a, b):
    return lax.dot_general(a, b, (((1,), (1,)), ((), ())), preferred_element_type=F32)


def halves(x):
    high = x.astype(BF16).astype(F32)
    return high, (x - high).astype(BF16).astype(F32)


def spread(row, rows):
    n = row.shape[1]
    block = jnp.broadcast_to(row, (16, n)).astype(BF16)
    return jnp.broadcast_to(block[None], (rows // 16, 16, n))


def counter(rows, n):
    return (
        (lax.broadcasted_iota(jnp.int32, (rows // 16, 16, n), 0) * 16
         + lax.broadcasted_iota(jnp.int32, (rows // 16, 16, n), 1)).astype(F32).astype(BF16)
    )


def hot(row, rows):
    n = row.shape[1]
    mask = counter(rows, n) == spread(row, rows)
    return jnp.where(mask, BF16(1), BF16(0)).reshape(rows, n)


def hot_values(row, values, rows):
    n = row.shape[1]
    mask = counter(rows, n) == spread(row, rows)
    return [
        jnp.where(mask, spread(v, rows), jnp.zeros((rows // 16, 16, n), BF16)).reshape(rows, n)
        for v in values
    ]


def hot512(row):
    return hot(row, 256), hot(row - 256.0, 256)


def divide(x, by):
    whole = jnp.floor(x * (1.0 / by))
    return whole, x - whole * by


def harmonic(first, second):
    return 2.0 * first * second / (first + second)


def slots(own_ref, count, rows, q_out, lane_out, hot_own, tri):
    n = count * D

    def build(c, carry):
        at = pl.ds(pl.multiple_of(c * D, D), D)
        hot_own[:, at] = hot(own_ref[pl.ds(c, 1), :].astype(F32), D)
        return carry

    lax.fori_loop(0, count, build, 0, unroll=4)
    earlier = lax.broadcasted_iota(jnp.int32, (n, D), 0) // 256 < lax.broadcasted_iota(jnp.int32, (n, D), 1)
    base = dot_nn(hot_own[:, 0:n], jnp.where(earlier, 1.0, 0.0).astype(BF16))
    for c in range(count // 2):
        upto = dot_nn(hot_own[:, c * 256:(c + 1) * 256], tri[...])
        before = jnp.broadcast_to(base[:, c:c + 1], (D, D))
        for h in range(2):
            own = own_ref[2 * c + h:2 * c + h + 1, :]
            mask = lax.broadcasted_iota(jnp.int32, (D, D), 0) == own
            rank = jnp.sum(jnp.where(mask, upto[:, h * D:(h + 1) * D] + before, 0.0), axis=0, keepdims=True) - 1.0
            block, rest = divide(own.astype(F32), rows)
            q_out[2 * c + h:2 * c + h + 1, :] = rest
            lane_out[2 * c + h:2 * c + h + 1, :] = block * rows + rank


def pack(count, rows, values_of, planes, own_q, own_slot):
    lanes, values = [], []
    for c in range(count):
        lanes.append(hot(own_slot[c:c + 1, :], D))
        values.append(jnp.concatenate(hot_values(own_q[c:c + 1, :], values_of(c), rows), axis=0))
    out = dot_nt(jnp.concatenate(values, axis=1), jnp.concatenate(lanes, axis=1))
    return [out[p * rows:(p + 1) * rows, :] for p in range(planes)]


def gather(table, hots, j_ref, chunks, out):
    for c in range(chunks // 2):
        got = dot_nn(table[...], hots[:, c * 256:(c + 1) * 256])
        both = got[0:D, :] + got[D:2 * D, :]
        for h in range(2):
            k = 2 * c + h
            mask = lax.broadcasted_iota(jnp.int32, (D, D), 0) == j_ref[k:k + 1, :].astype(jnp.int32)
            out(k, jnp.sum(jnp.where(mask, both[:, h * D:(h + 1) * D], 0.0), axis=0, keepdims=True))


def scatter(values, hots, j_ref, chunks, width=16):
    total = None
    for start in range(0, chunks, width):
        parts = []
        for c in range(start, start + width):
            rows = []
            for v in values:
                rows.extend(halves(v[c:c + 1, :]))
            parts.append(jnp.concatenate(hot_values(j_ref[c:c + 1, :], rows, D), axis=0))
        part = dot_nt(jnp.concatenate(parts, axis=1), hots[:, start * D:(start + width) * D])
        total = part if total is None else total + part
    return [total[2 * p * D:(2 * p + 1) * D, :] + total[(2 * p + 1) * D:(2 * p + 2) * D, :] for p in range(len(values))]


def build512(r_ref, hots, chunks):
    def chunk(c, carry):
        at = pl.ds(pl.multiple_of(c * D, D), D)
        low, high = hot512(r_ref[pl.ds(c, 1), :])
        hots[0:256, at] = low
        hots[256:512, at] = high
        return carry

    lax.fori_loop(0, chunks, chunk, 0, unroll=4)


def set_table(tbl, q):
    high, low = halves(q)
    tbl[0:D, :] = high.astype(BF16)
    tbl[D:2 * D, :] = low.astype(BF16)


def kernel(
    mp, perm, stor, fp, ia, ns,
    icell, iown, ifrac, iseg, wi,
    jfrac, jseg, jown, jffrac, jfseg, jtrans,
    fnew, mnew,
    hot_own, col_hot, own_slot, own_q,
    tri,
    near_r, near_j, near_t, served_r, served_j, isr_r, isr_j, isr_w, isr_ws, cell_r, cell_c, cell_w,
    work, rhot_srv, rhot_near, rhot_is, rhot_cells, tbl,
    q_now, cn, cs, cw, ce, inv, sto, apt, m_tot, m_wts,
    jsend, jrecv, isend, irecv, asend, arecv, rsend, rrecv, hsend, hrecv,
    send_sem, recv_sem, hsend_sem, hrecv_sem,
):
    gx = lax.axis_index("gx")
    gy = lax.axis_index("gy")
    me = gx * 8 + gy
    bar = pltpu.get_barrier_semaphore()

    def greet(k, c):
        pl.semaphore_signal(bar, inc=1, device_id=lax.rem(me + k, D), device_id_type=LOGICAL)
        return c

    lax.fori_loop(1, D, greet, 0)

    def exchange(number, src, dst, rows):
        def send(k, c):
            t = lax.rem(me + (D // 2) + k, D)
            pltpu.make_async_remote_copy(
                src.at[lax.rem(t, rows)], dst.at[me], send_sem.at[number], recv_sem.at[number],
                device_id=t, device_id_type=LOGICAL,
            ).start()
            return c

        lax.fori_loop(0, D // 2, send, 0)
        lax.fori_loop(D // 2 + 1, D, send, 0)
        pltpu.make_async_copy(src.at[lax.rem(me, rows)], dst.at[me], recv_sem.at[number]).start()

    def arrived(number, dst):
        pltpu.make_async_copy(dst, dst, recv_sem.at[number]).wait()

    def sent(number, dst):
        part = dst.at[pl.ds(0, D - 1)]
        pltpu.make_async_copy(part, part, send_sem.at[number]).wait()

    def merge(got, rows):
        blocks = D // rows
        width = D // blocks
        mine = me // rows
        lane_block = lax.broadcasted_iota(jnp.int32, (rows, D), 1) // width
        out = jnp.zeros((rows, D), F32)
        for k in range(blocks):
            part = pltpu.roll(got[k * rows:(k + 1) * rows, :], lax.rem((k - mine + blocks) * width, D), 1)
            out = jnp.where(lane_block == k, part, out)
        return out

    tri[...] = jnp.where(
        lax.broadcasted_iota(jnp.int32, (256, 256), 0) <= lax.broadcasted_iota(jnp.int32, (256, 256), 1), 1.0, 0.0
    ).astype(BF16)

    slots(jown, 16, QJ, own_q, own_slot, hot_own, tri)

    def requests(c):
        high, low = divide((jffrac[c:c + 1, :] * (D * D) + jfseg[c:c + 1, :]).astype(F32), 256)
        nigh, nlow = divide((jfrac[c:c + 1, :] * (D * D) + jseg[c:c + 1, :]).astype(F32), 256)
        t_high, t_low = halves(jtrans[c:c + 1, :])
        return [high * 256.0, low, nigh * 256.0, nlow, t_high, t_low]

    r_high, r_low, n_high, n_low, t_high, t_low = pack(16, QJ, requests, 6, own_q, own_slot)
    jsend[:, 0, :] = r_high + r_low
    row, col = divide(n_high + n_low, D)
    near_r[...] = row
    near_j[...] = col
    near_t[...] = t_high + t_low
    pl.semaphore_wait(bar, D - 1)
    exchange(0, jsend, jrecv, QJ)

    p_high, p_low = halves(mp[...])
    work[0:D, :] = p_high.astype(BF16)
    work[D:2 * D, :] = p_low.astype(BF16)

    def cell_hots(c, carry):
        unused, col = divide(icell[pl.ds(c, 1), :].astype(F32), 256)
        col_hot[:, pl.ds(pl.multiple_of(c * D, D), D)] = hot(col, 256)
        cell_r[pl.ds(c, 1), :] = unused
        return carry

    lax.fori_loop(0, 32, cell_hots, 0, unroll=4)

    def keep_sample(c, row):
        isr_ws[c:c + 1, :] = row * wi[c:c + 1, :]

    gather(work, col_hot, cell_r, 32, keep_sample)
    slots(iown, 32, QI, own_q, own_slot, hot_own, tri)

    def wells(c):
        high, low = divide((ifrac[c:c + 1, :] * (D * D) + iseg[c:c + 1, :]).astype(F32), 256)
        c_high, c_low = divide(icell[c:c + 1, :].astype(F32), 256)
        w_high, w_low = halves(wi[c:c + 1, :])
        s_high, s_low = halves(isr_ws[c:c + 1, :])
        return [high * 256.0, low, w_high, w_low, s_high, s_low, c_high, c_low]

    i_high, i_low, w_high, w_low, s_high, s_low, c_high, c_low = pack(32, QI, wells, 8, own_q, own_slot)
    isend[:, 0, 0, :] = i_high + i_low
    isend[:, 1, 0, :] = w_high + w_low
    isend[:, 2, 0, :] = s_high + s_low
    exchange(1, isend, irecv, QI)
    cell_r[...] = c_high
    cell_c[...] = c_low
    cell_w[...] = w_high + w_low

    for f in range(4):
        at = slice(f * D, (f + 1) * D)
        p0 = fp[f].T
        effective = ns[f].T - p0
        q_now[:, at] = p0
        apt[:, at] = ia[f].T - 0.5 * effective / (0.5 + effective)
    set_table(tbl, q_now[...])

    def answer(round_number):
        def keep(c, row):
            asend[round_number, c:c + 1, 0, :] = row

        gather(tbl, rhot_srv, served_j, QJ, keep)
        exchange(2 + round_number, asend.at[round_number], arecv.at[round_number], QJ)

    arrived(0, jrecv)
    row, col = divide(merge(jrecv[:, 0, :], QJ), D)
    served_r[...] = row
    served_j[...] = col
    build512(served_r, rhot_srv, QJ)
    answer(0)

    build512(near_r, rhot_near, QJ)
    (junc_diag,) = scatter([near_t], rhot_near, near_j, QJ)
    inv[...] = junc_diag
    arrived(1, irecv)
    row, col = divide(merge(irecv[:, 0, 0, :], QI), D)
    isr_r[...] = row
    isr_j[...] = col
    isr_w[...] = merge(irecv[:, 1, 0, :], QI)
    isr_ws[...] = merge(irecv[:, 2, 0, :], QI)
    build512(isr_r, rhot_is, QI)
    diag, rhs = scatter([isr_w, isr_ws], rhot_is, isr_j, QI)
    inv[...] += diag
    sto[...] = rhs
    lane = lax.broadcasted_iota(jnp.int32, (D, D), 1)
    sub = lax.broadcasted_iota(jnp.int32, (D, D), 0)
    for f in range(4):
        at = slice(f * D, (f + 1) * D)
        ap = apt[:, at]
        cond = ap * ap * ap
        north = jnp.where(lane == 0, 0.0, harmonic(cond, pltpu.roll(cond, 1, 1)))
        south = jnp.where(lane == D - 1, 0.0, harmonic(cond, pltpu.roll(cond, D - 1, 1)))
        west = jnp.where(sub == 0, 0.0, harmonic(cond, pltpu.roll(cond, 1, 0)))
        east = jnp.where(sub == D - 1, 0.0, harmonic(cond, pltpu.roll(cond, D - 1, 0)))
        one = 1.0 / (ap + north + south + west + east + inv[:, at])
        inv[:, at] = one
        cn[:, at] = north * one
        cs[:, at] = south * one
        cw[:, at] = west * one
        ce[:, at] = east * one
        sto[:, at] = (ap * q_now[:, at] + sto[:, at]) * one

    def sweep(round_number):
        arrived(2 + round_number, arecv.at[round_number])
        served_r[...] = merge(arecv[round_number, :, 0, :], QJ) * near_t[...]
        (joined,) = scatter([served_r], rhot_near, near_j, QJ)
        for f in range(4):
            at = slice(f * D, (f + 1) * D)
            q = q_now[:, at]
            q_now[:, at] = (
                sto[:, at]
                + cn[:, at] * pltpu.roll(q, 1, 1)
                + cs[:, at] * pltpu.roll(q, D - 1, 1)
                + cw[:, at] * pltpu.roll(q, 1, 0)
                + ce[:, at] * pltpu.roll(q, D - 1, 0)
                + inv[:, at] * joined[:, at]
            )
        set_table(tbl, q_now[...])

    sweep(0)
    answer(1)

    hsend[0, 0, 0, :] = mp[0, 0:D]
    hsend[0, 1, 0, :] = mp[0, D:2 * D]
    hsend[0, 2, 0, :] = perm[0, 0:D]
    hsend[0, 3, 0, :] = perm[0, D:2 * D]
    hsend[1, 0, 0, :] = mp[D - 1, 0:D]
    hsend[1, 1, 0, :] = mp[D - 1, D:2 * D]
    hsend[1, 2, 0, :] = perm[D - 1, 0:D]
    hsend[1, 3, 0, :] = perm[D - 1, D:2 * D]
    mp_left = mp[:, 0:D].T
    mp_right = mp[:, D:2 * D].T
    perm_left = perm[:, 0:D].T
    perm_right = perm[:, D:2 * D].T
    hsend[2, 0, 0, :] = mp_left[0, :]
    hsend[2, 2, 0, :] = perm_left[0, :]
    hsend[3, 0, 0, :] = mp_right[D - 1, :]
    hsend[3, 2, 0, :] = perm_right[D - 1, :]
    hsend[2, 1, 0, :] = mp_left[0, :]
    hsend[2, 3, 0, :] = perm_left[0, :]
    hsend[3, 1, 0, :] = mp_right[D - 1, :]
    hsend[3, 3, 0, :] = perm_right[D - 1, :]
    targets = (
        lax.rem(gx + 15, 16) * 8 + gy,
        lax.rem(gx + 1, 16) * 8 + gy,
        gx * 8 + lax.rem(gy + 7, 8),
        gx * 8 + lax.rem(gy + 1, 8),
    )
    halo = [
        pltpu.make_async_remote_copy(
            hsend.at[n], hrecv.at[n], hsend_sem.at[n], hrecv_sem.at[n], device_id=t, device_id_type=LOGICAL
        )
        for n, t in enumerate(targets)
    ]
    for copy in halo:
        copy.start()
    def cell_slots(c, carry):
        at = pl.ds(pl.multiple_of(c * D, D), D)
        rhot_cells[:, at] = hot(cell_c[pl.ds(c, 1), :], 256)
        return carry

    lax.fori_loop(0, QI, cell_slots, 0, unroll=4)
    (m_diag,) = scatter([cell_w], rhot_cells, cell_r, QI)
    m_wts[...] = stor[...] + m_diag

    sweep(1)
    answer(2)

    for copy in halo:
        copy.wait()
    press, k = mp[...], perm[...]
    rows = lax.broadcasted_iota(jnp.int32, (D, 256), 0)
    cols = lax.broadcasted_iota(jnp.int32, (D, 256), 1)

    def wide(n, plane):
        return jnp.concatenate([hrecv[n, plane], hrecv[n, plane + 1]], axis=1)

    def tall(n, plane):
        column = jnp.broadcast_to(hrecv[n, plane], (D, D)).T
        return jnp.concatenate([column, column], axis=1)

    total = stor[...] * press
    weights = m_wts[...]
    for n, shift, axis, at_edge, outside in (
        (1, 1, 0, rows == 0, gx == 0),
        (0, D - 1, 0, rows == D - 1, gx == 15),
        (3, 1, 1, cols == 0, gy == 0),
        (2, 255, 1, cols == 255, gy == 7),
    ):
        far_p = wide(n, 0) if axis == 0 else tall(n, 0)
        far_k = wide(n, 2) if axis == 0 else tall(n, 2)
        beside_p = jnp.where(at_edge, far_p, pltpu.roll(press, shift, axis))
        beside_k = jnp.where(at_edge, far_k, pltpu.roll(k, shift, axis))
        gone = jnp.where(outside, 0.0, 1.0)
        face = harmonic(k, beside_k) * jnp.where(at_edge, gone, 1.0)
        total = total + face * beside_p
        weights = weights + face
    m_tot[...] = total
    m_wts[...] = weights

    sweep(2)

    def keep_reply(c, row):
        rsend[c:c + 1, 0, :] = row

    gather(tbl, rhot_is, isr_j, QI, keep_reply)
    exchange(5, rsend, rrecv, QI)
    for f in range(4):
        fnew[f] = q_now[:, f * D:(f + 1) * D].T
    arrived(5, rrecv)
    isr_ws[...] = merge(rrecv[:, 0, :], QI) * cell_w[...]
    (m_rhs,) = scatter([isr_ws], rhot_cells, cell_r, QI)
    mnew[...] = (m_tot[...] + m_rhs) / m_wts[...]

    sent(0, jrecv)
    sent(1, irecv)
    for n in range(SWEEPS):
        sent(2 + n, arecv.at[n])
    sent(5, rrecv)


def shards(
    matrix_pressure, permeability, matrix_storage, fracture_pressure, initial_aperture, normal_stress,
    isect_cell, isect_owner, isect_frac, isect_seg, well_index,
    junc_frac, junc_seg, junc_owner, junc_far_frac, junc_far_seg, junc_trans,
):
    lanes = [
        a.reshape(-1, D)
        for a in (
            isect_cell, isect_owner, isect_frac, isect_seg, well_index,
            junc_frac, junc_seg, junc_owner, junc_far_frac, junc_far_seg, junc_trans,
        )
    ]
    vm = pltpu.VMEM
    scratch = [
        vm((D, 4096), BF16),
        vm((256, 4096), BF16),
        vm((QI, D), F32),
        vm((QI, D), F32),
        vm((256, 256), BF16),
    ]
    scratch += [vm((QJ, D), F32)] * 5
    scratch += [vm((QI, D), F32)] * 7
    scratch += [
        vm((256, 256), BF16),
        vm((512, 4096), BF16),
        vm((512, 4096), BF16),
        vm((512, 8192), BF16),
        vm((256, 8192), BF16),
        vm((256, 512), BF16),
    ]
    scratch += [vm((D, 512), F32)] * 8
    scratch += [vm((D, 256), F32)] * 2
    scratch += [
        vm((QJ, 1, D), F32),
        vm((D, 1, D), F32),
        vm((QI, 3, 1, D), F32),
        vm((D, 3, 1, D), F32),
        vm((SWEEPS, QJ, 1, D), F32),
        vm((SWEEPS, D, 1, D), F32),
        vm((QI, 1, D), F32),
        vm((D, 1, D), F32),
        vm((4, 4, 1, D), F32),
        vm((4, 4, 1, D), F32),
        pltpu.SemaphoreType.DMA((6,)),
        pltpu.SemaphoreType.DMA((6,)),
        pltpu.SemaphoreType.DMA((4,)),
        pltpu.SemaphoreType.DMA((4,)),
    ]
    return pl.pallas_call(
        kernel,
        out_shape=(
            jax.ShapeDtypeStruct(fracture_pressure.shape, F32),
            jax.ShapeDtypeStruct(matrix_pressure.shape, F32),
        ),
        in_specs=[pl.BlockSpec(memory_space=pltpu.VMEM)] * 17,
        out_specs=(pl.BlockSpec(memory_space=pltpu.VMEM),) * 2,
        scratch_shapes=scratch,
        compiler_params=pltpu.CompilerParams(
            collective_id=0, has_side_effects=True, vmem_limit_bytes=60 << 20
        ),
    )(matrix_pressure, permeability, matrix_storage, fracture_pressure, initial_aperture, normal_stress, *lanes)


def solution(mesh):
    in_specs = (
        (P("gx", "gy"),) * 3
        + (P(("gx", "gy"), None, None),) * 3
        + (P(("gx", "gy")), P(("gx", "gy"), None), P(("gx", "gy")), P(("gx", "gy")), P(("gx", "gy")))
        + (P(("gx", "gy")), P(("gx", "gy")), P(("gx", "gy"), None), P(("gx", "gy")), P(("gx", "gy")), P(("gx", "gy")))
    )
    out_specs = (P(("gx", "gy"), None, None), P("gx", "gy"))
    return jax.shard_map(shards, mesh=mesh, in_specs=in_specs, out_specs=out_specs, check_vma=False)
```

```python
import jax
import jax.numpy as jnp
from jax import lax
from jax.experimental import pallas as pl
from jax.experimental.pallas import tpu as pltpu
from jax.sharding import PartitionSpec as P

LOGICAL = pl.DeviceIdType.LOGICAL
LOAD_ORDER = (13, 14, 15, 11, 12, 16, 6, 0, 7, 8, 9, 10, 3, 5, 4, 1, 2)
F32 = jnp.float32
BF16 = jnp.bfloat16
SWEEPS = 3
D = 128
QJ = 32
QI = 64


def ring(d):
    return min(d, 4 - d)


ORDER = sorted(
    [(dy, dx, dz, dc) for dy in range(4) for dx in range(4) for dz in range(4) for dc in range(2)][1:],
    key=lambda v: -(ring(v[0]) + ring(v[1]) + ring(v[2])),
)


def dot_nn(a, b):
    return lax.dot_general(a, b, (((1,), (0,)), ((), ())), preferred_element_type=F32)


def dot_nt(a, b):
    return lax.dot_general(a, b, (((1,), (1,)), ((), ())), preferred_element_type=F32)


def halves(x):
    high = x.astype(BF16).astype(F32)
    return high, (x - high).astype(BF16).astype(F32)


def spread(row, rows):
    n = row.shape[1]
    block = jnp.broadcast_to(row, (16, n)).astype(BF16)
    return jnp.broadcast_to(block[None], (rows // 16, 16, n))


def counter(rows, n):
    return (
        (lax.broadcasted_iota(jnp.int32, (rows // 16, 16, n), 0) * 16
         + lax.broadcasted_iota(jnp.int32, (rows // 16, 16, n), 1)).astype(F32).astype(BF16)
    )


def hot(row, rows):
    n = row.shape[1]
    mask = counter(rows, n) == spread(row, rows)
    return jnp.where(mask, BF16(1), BF16(0)).reshape(rows, n)


def hot_values(row, values, rows):
    n = row.shape[1]
    mask = counter(rows, n) == spread(row, rows)
    return [
        jnp.where(mask, spread(v, rows), jnp.zeros((rows // 16, 16, n), BF16)).reshape(rows, n)
        for v in values
    ]


def divide(x, by):
    whole = jnp.floor(x * (1.0 / by))
    return whole, x - whole * by


def harmonic(first, second):
    return 2.0 * first * second / (first + second)


def slots(own_ref, count, rows, q_out, lane_out, hot_own, tri):
    n = count * D

    def build(c, carry):
        at = pl.ds(pl.multiple_of(c * D, D), D)
        hot_own[:, at] = hot(own_ref[pl.ds(c, 1), :].astype(F32), D)
        return carry

    lax.fori_loop(0, count, build, 0, unroll=4)
    earlier = lax.broadcasted_iota(jnp.int32, (n, D), 0) // 256 < lax.broadcasted_iota(jnp.int32, (n, D), 1)
    base = dot_nn(hot_own[:, 0:n], jnp.where(earlier, 1.0, 0.0).astype(BF16))
    for c in range(count // 2):
        upto = dot_nn(hot_own[:, c * 256:(c + 1) * 256], tri[...])
        before = jnp.broadcast_to(base[:, c:c + 1], (D, D))
        for h in range(2):
            own = own_ref[2 * c + h:2 * c + h + 1, :]
            mask = lax.broadcasted_iota(jnp.int32, (D, D), 0) == own
            rank = jnp.sum(jnp.where(mask, upto[:, h * D:(h + 1) * D] + before, 0.0), axis=0, keepdims=True) - 1.0
            block, rest = divide(own.astype(F32), rows)
            q_out[2 * c + h:2 * c + h + 1, :] = rest
            lane_out[2 * c + h:2 * c + h + 1, :] = block * rows + rank


def pack(count, rows, values_of, planes, own_q, own_slot):
    lanes, values = [], []
    for c in range(count):
        lanes.append(hot(own_slot[c:c + 1, :], D))
        values.append(jnp.concatenate(hot_values(own_q[c:c + 1, :], values_of(c), rows), axis=0))
    out = dot_nt(jnp.concatenate(values, axis=1), jnp.concatenate(lanes, axis=1))
    return [out[p * rows:(p + 1) * rows, :] for p in range(planes)]


def columns(row, rows):
    if rows == 256:
        return hot(row, 256)
    return jnp.concatenate([hot(row, 256), hot(row - 256.0, 256)], axis=0)


def gather(table, hots, j_ref, chunks, out, r_ref=None):
    for c in range(chunks // 2):
        at = slice(c * 256, (c + 1) * 256)
        if r_ref is None:
            cols = hots[:, at]
        else:
            cols = jnp.concatenate([columns(r_ref[k:k + 1, :], table.shape[1]) for k in (2 * c, 2 * c + 1)], axis=1)
            if hots is not None:
                hots[:, at] = cols
        got = dot_nn(table[...], cols)
        both = got[0:D, :] + got[D:2 * D, :]
        for h in range(2):
            k = 2 * c + h
            mask = lax.broadcasted_iota(jnp.int32, (D, D), 0) == j_ref[k:k + 1, :].astype(jnp.int32)
            out(k, jnp.sum(jnp.where(mask, both[:, h * D:(h + 1) * D], 0.0), axis=0, keepdims=True))


def scatter(values, hots, j_ref, chunks, r_ref=None, width=16):
    total = None
    for start in range(0, chunks, width):
        parts, made = [], []
        at = slice(start * D, (start + width) * D)
        for c in range(start, start + width):
            rows = []
            for v in values:
                rows.extend(halves(v[c:c + 1, :]))
            parts.append(jnp.concatenate(hot_values(j_ref[c:c + 1, :], rows, D), axis=0))
            if r_ref is not None:
                made.append(columns(r_ref[c:c + 1, :], hots.shape[0]))
        if r_ref is None:
            cols = hots[:, at]
        else:
            cols = jnp.concatenate(made, axis=1)
            hots[:, at] = cols
        part = dot_nt(jnp.concatenate(parts, axis=1), cols)
        total = part if total is None else total + part
    return [total[2 * p * D:(2 * p + 1) * D, :] + total[(2 * p + 1) * D:(2 * p + 2) * D, :] for p in range(len(values))]


def set_table(tbl, q):
    high, low = halves(q)
    tbl[0:D, :] = high.astype(BF16)
    tbl[D:2 * D, :] = low.astype(BF16)


def kernel(*refs):
    given, (fnew, mnew), held = refs[0:17], refs[17:19], refs[19:36]
    (
        mp, perm, stor, fp, ia, ns,
        icell, iown, ifrac, iseg, wi,
        jfrac, jseg, jown, jffrac, jfseg, jtrans,
    ) = held
    (
        hot_own, own_slot, own_q, tri,
        near_r, near_j, near_t, served_r, served_j, isr_r, isr_j, isr_w, isr_ws, cell_r, cell_c, cell_w,
        work, rhot_srv, rhot_near, rhot_is, rhot_cells, tbl,
        q_now, cn, cs, cw, ce, inv, sto, apt, m_tot, m_wts,
        jsend, jrecv, isend, irecv, asend, arecv, rsend, rrecv, hsend, hrecv,
        load_sem, send_sem, recv_sem, hsend_sem, hrecv_sem,
    ) = refs[36:]
    gx = lax.axis_index("gx")
    gy = lax.axis_index("gy")
    me = gx * 8 + gy
    y, x, z, core = gx // 4, lax.rem(gx, 4), gy // 2, lax.rem(gy, 2)

    def peer(v):
        return (lax.rem(y + v[0], 4) * 4 + lax.rem(x + v[1], 4)) * 8 + lax.rem(z + v[2], 4) * 2 + lax.rem(core + v[3], 2)

    loads = [pltpu.make_async_copy(a, b, load_sem.at[n]) for n, (a, b) in enumerate(zip(given, held))]
    for n in LOAD_ORDER:
        loads[n].start()
    bar = pltpu.get_barrier_semaphore()
    for v in ORDER:
        pl.semaphore_signal(bar, inc=1, device_id=peer(v), device_id_type=LOGICAL)

    def ready(*numbers):
        for n in numbers:
            loads[n].wait()

    def exchange(number, src, dst, rows):
        for v in ORDER:
            t = peer(v)
            pltpu.make_async_remote_copy(
                src.at[lax.rem(t, rows)], dst.at[me], send_sem.at[number], recv_sem.at[number],
                device_id=t, device_id_type=LOGICAL,
            ).start()
        pltpu.make_async_copy(src.at[lax.rem(me, rows)], dst.at[me], recv_sem.at[number]).start()

    def arrived(number, dst):
        pltpu.make_async_copy(dst, dst, recv_sem.at[number]).wait()

    def sent(number, dst):
        part = dst.at[pl.ds(0, D - 1)]
        pltpu.make_async_copy(part, part, send_sem.at[number]).wait()

    def merge(got, rows):
        blocks = D // rows
        width = D // blocks
        mine = me // rows
        lane_block = lax.broadcasted_iota(jnp.int32, (rows, D), 1) // width
        out = jnp.zeros((rows, D), F32)
        for k in range(blocks):
            part = pltpu.roll(got[k * rows:(k + 1) * rows, :], lax.rem((k - mine + blocks) * width, D), 1)
            out = jnp.where(lane_block == k, part, out)
        return out

    tri[...] = jnp.where(
        lax.broadcasted_iota(jnp.int32, (256, 256), 0) <= lax.broadcasted_iota(jnp.int32, (256, 256), 1), 1.0, 0.0
    ).astype(BF16)

    ready(13)
    slots(jown, 16, QJ, own_q, own_slot, hot_own, tri)

    def requests(c):
        high, low = divide((jffrac[c:c + 1, :] * (D * D) + jfseg[c:c + 1, :]).astype(F32), 256)
        nigh, nlow = divide((jfrac[c:c + 1, :] * (D * D) + jseg[c:c + 1, :]).astype(F32), 256)
        t_high, t_low = halves(jtrans[c:c + 1, :])
        return [high * 256.0, low, nigh * 256.0, nlow, t_high, t_low]

    ready(11, 12, 14, 15, 16)
    r_high, r_low, n_high, n_low, t_high, t_low = pack(16, QJ, requests, 6, own_q, own_slot)
    jsend[:, 0, :] = r_high + r_low
    row, col = divide(n_high + n_low, D)
    near_r[...] = row
    near_j[...] = col
    near_t[...] = t_high + t_low
    pl.semaphore_wait(bar, D - 1)
    exchange(0, jsend, jrecv, QJ)

    ready(0, 6, 7, 8, 9, 10)
    p_high, p_low = halves(mp[...])
    work[0:D, :] = p_high.astype(BF16)
    work[D:2 * D, :] = p_low.astype(BF16)

    row, col = divide(icell[...].astype(F32), 256)
    cell_r[0:32, :] = row
    cell_c[0:32, :] = col

    def keep_sample(c, row):
        isr_ws[c:c + 1, :] = row * wi[c:c + 1, :]

    gather(work, None, cell_r, 32, keep_sample, cell_c)
    slots(iown, 32, QI, own_q, own_slot, hot_own, tri)

    def wells(c):
        high, low = divide((ifrac[c:c + 1, :] * (D * D) + iseg[c:c + 1, :]).astype(F32), 256)
        c_high, c_low = divide(icell[c:c + 1, :].astype(F32), 256)
        w_high, w_low = halves(wi[c:c + 1, :])
        s_high, s_low = halves(isr_ws[c:c + 1, :])
        return [high * 256.0, low, w_high, w_low, s_high, s_low, c_high, c_low]

    i_high, i_low, w_high, w_low, s_high, s_low, c_high, c_low = pack(32, QI, wells, 8, own_q, own_slot)
    isend[:, 0, 0, :] = i_high + i_low
    isend[:, 1, 0, :] = w_high + w_low
    isend[:, 2, 0, :] = s_high + s_low
    exchange(1, isend, irecv, QI)
    cell_r[...] = c_high
    cell_c[...] = c_low
    cell_w[...] = w_high + w_low

    ready(3, 4, 5)
    for f in range(4):
        at = slice(f * D, (f + 1) * D)
        p0 = fp[f].T
        effective = ns[f].T - p0
        q_now[:, at] = p0
        apt[:, at] = ia[f].T - 0.5 * effective / (0.5 + effective)
    set_table(tbl, q_now[...])

    (junc_diag,) = scatter([near_t], rhot_near, near_j, QJ, near_r)
    inv[...] = junc_diag

    def answer(round_number):
        def keep(c, row):
            asend[round_number, c:c + 1, 0, :] = row

        gather(tbl, rhot_srv, served_j, QJ, keep, served_r if round_number == 0 else None)
        exchange(2 + round_number, asend.at[round_number], arecv.at[round_number], QJ)

    arrived(0, jrecv)
    row, col = divide(merge(jrecv[:, 0, :], QJ), D)
    served_r[...] = row
    served_j[...] = col
    answer(0)

    arrived(1, irecv)
    row, col = divide(merge(irecv[:, 0, 0, :], QI), D)
    isr_r[...] = row
    isr_j[...] = col
    isr_w[...] = merge(irecv[:, 1, 0, :], QI)
    isr_ws[...] = merge(irecv[:, 2, 0, :], QI)
    diag, rhs = scatter([isr_w, isr_ws], rhot_is, isr_j, QI, isr_r)
    inv[...] += diag
    sto[...] = rhs
    lane = lax.broadcasted_iota(jnp.int32, (D, D), 1)
    sub = lax.broadcasted_iota(jnp.int32, (D, D), 0)
    for f in range(4):
        at = slice(f * D, (f + 1) * D)
        ap = apt[:, at]
        cond = ap * ap * ap
        north = jnp.where(lane == 0, 0.0, harmonic(cond, pltpu.roll(cond, 1, 1)))
        south = jnp.where(lane == D - 1, 0.0, harmonic(cond, pltpu.roll(cond, D - 1, 1)))
        west = jnp.where(sub == 0, 0.0, harmonic(cond, pltpu.roll(cond, 1, 0)))
        east = jnp.where(sub == D - 1, 0.0, harmonic(cond, pltpu.roll(cond, D - 1, 0)))
        one = 1.0 / (ap + north + south + west + east + inv[:, at])
        inv[:, at] = one
        cn[:, at] = north * one
        cs[:, at] = south * one
        cw[:, at] = west * one
        ce[:, at] = east * one
        sto[:, at] = (ap * q_now[:, at] + sto[:, at]) * one

    def sweep(round_number):
        arrived(2 + round_number, arecv.at[round_number])
        served_r[...] = merge(arecv[round_number, :, 0, :], QJ) * near_t[...]
        (joined,) = scatter([served_r], rhot_near, near_j, QJ)
        for f in range(4):
            at = slice(f * D, (f + 1) * D)
            q = q_now[:, at]
            q_now[:, at] = (
                sto[:, at]
                + cn[:, at] * pltpu.roll(q, 1, 1)
                + cs[:, at] * pltpu.roll(q, D - 1, 1)
                + cw[:, at] * pltpu.roll(q, 1, 0)
                + ce[:, at] * pltpu.roll(q, D - 1, 0)
                + inv[:, at] * joined[:, at]
            )
        set_table(tbl, q_now[...])

    sweep(0)
    answer(1)

    ready(1, 2)
    hsend[0, 0, 0, :] = mp[0, 0:D]
    hsend[0, 1, 0, :] = mp[0, D:2 * D]
    hsend[0, 2, 0, :] = perm[0, 0:D]
    hsend[0, 3, 0, :] = perm[0, D:2 * D]
    hsend[1, 0, 0, :] = mp[D - 1, 0:D]
    hsend[1, 1, 0, :] = mp[D - 1, D:2 * D]
    hsend[1, 2, 0, :] = perm[D - 1, 0:D]
    hsend[1, 3, 0, :] = perm[D - 1, D:2 * D]
    mp_left = mp[:, 0:D].T
    mp_right = mp[:, D:2 * D].T
    perm_left = perm[:, 0:D].T
    perm_right = perm[:, D:2 * D].T
    hsend[2, 0, 0, :] = mp_left[0, :]
    hsend[2, 2, 0, :] = perm_left[0, :]
    hsend[3, 0, 0, :] = mp_right[D - 1, :]
    hsend[3, 2, 0, :] = perm_right[D - 1, :]
    hsend[2, 1, 0, :] = mp_left[0, :]
    hsend[2, 3, 0, :] = perm_left[0, :]
    hsend[3, 1, 0, :] = mp_right[D - 1, :]
    hsend[3, 3, 0, :] = perm_right[D - 1, :]
    targets = (
        lax.rem(gx + 15, 16) * 8 + gy,
        lax.rem(gx + 1, 16) * 8 + gy,
        gx * 8 + lax.rem(gy + 7, 8),
        gx * 8 + lax.rem(gy + 1, 8),
    )
    halo = [
        pltpu.make_async_remote_copy(
            hsend.at[n], hrecv.at[n], hsend_sem.at[n], hrecv_sem.at[n], device_id=t, device_id_type=LOGICAL
        )
        for n, t in enumerate(targets)
    ]
    for copy in halo:
        copy.start()
    (m_diag,) = scatter([cell_w], rhot_cells, cell_r, QI, cell_c)
    m_wts[...] = stor[...] + m_diag

    sweep(1)
    answer(2)

    for copy in halo:
        copy.wait()
    press, k = mp[...], perm[...]
    rows = lax.broadcasted_iota(jnp.int32, (D, 256), 0)
    cols = lax.broadcasted_iota(jnp.int32, (D, 256), 1)

    def wide(n, plane):
        return jnp.concatenate([hrecv[n, plane], hrecv[n, plane + 1]], axis=1)

    def tall(n, plane):
        column = jnp.broadcast_to(hrecv[n, plane], (D, D)).T
        return jnp.concatenate([column, column], axis=1)

    total = stor[...] * press
    weights = m_wts[...]
    for n, shift, axis, at_edge, outside in (
        (1, 1, 0, rows == 0, gx == 0),
        (0, D - 1, 0, rows == D - 1, gx == 15),
        (3, 1, 1, cols == 0, gy == 0),
        (2, 255, 1, cols == 255, gy == 7),
    ):
        far_p = wide(n, 0) if axis == 0 else tall(n, 0)
        far_k = wide(n, 2) if axis == 0 else tall(n, 2)
        beside_p = jnp.where(at_edge, far_p, pltpu.roll(press, shift, axis))
        beside_k = jnp.where(at_edge, far_k, pltpu.roll(k, shift, axis))
        gone = jnp.where(outside, 0.0, 1.0)
        face = harmonic(k, beside_k) * jnp.where(at_edge, gone, 1.0)
        total = total + face * beside_p
        weights = weights + face
    m_tot[...] = total
    m_wts[...] = weights

    sweep(2)

    def keep_reply(c, row):
        rsend[c:c + 1, 0, :] = row

    gather(tbl, rhot_is, isr_j, QI, keep_reply)
    exchange(5, rsend, rrecv, QI)
    for f in range(4):
        fnew[f] = q_now[:, f * D:(f + 1) * D].T
    arrived(5, rrecv)
    isr_ws[...] = merge(rrecv[:, 0, :], QI) * cell_w[...]
    (m_rhs,) = scatter([isr_ws], rhot_cells, cell_r, QI)
    mnew[...] = (m_tot[...] + m_rhs) / m_wts[...]

    sent(0, jrecv)
    sent(1, irecv)
    for n in range(SWEEPS):
        sent(2 + n, arecv.at[n])
    sent(5, rrecv)


def hand_over(a, b, a_out, b_out):
    a_out[...] = a[...]
    b_out[...] = b[...]


def shards(
    matrix_pressure, permeability, matrix_storage, fracture_pressure, initial_aperture, normal_stress,
    isect_cell, isect_owner, isect_frac, isect_seg, well_index,
    junc_frac, junc_seg, junc_owner, junc_far_frac, junc_far_seg, junc_trans,
):
    lanes = [
        a.reshape(-1, D)
        for a in (
            isect_cell, isect_owner, isect_frac, isect_seg, well_index,
            junc_frac, junc_seg, junc_owner, junc_far_frac, junc_far_seg, junc_trans,
        )
    ]
    vm = pltpu.VMEM
    args = (matrix_pressure, permeability, matrix_storage, fracture_pressure, initial_aperture, normal_stress, *lanes)
    scratch = [vm(a.shape, a.dtype) for a in args]
    scratch += [
        vm((D, 4096), BF16),
        vm((QI, D), F32),
        vm((QI, D), F32),
        vm((256, 256), BF16),
    ]
    scratch += [vm((QJ, D), F32)] * 5
    scratch += [vm((QI, D), F32)] * 7
    scratch += [
        vm((256, 256), BF16),
        vm((512, 4096), BF16),
        vm((512, 4096), BF16),
        vm((512, 8192), BF16),
        vm((256, 8192), BF16),
        vm((256, 512), BF16),
    ]
    scratch += [vm((D, 512), F32)] * 8
    scratch += [vm((D, 256), F32)] * 2
    scratch += [
        vm((QJ, 1, D), F32),
        vm((D, 1, D), F32),
        vm((QI, 3, 1, D), F32),
        vm((D, 3, 1, D), F32),
        vm((SWEEPS, QJ, 1, D), F32),
        vm((SWEEPS, D, 1, D), F32),
        vm((QI, 1, D), F32),
        vm((D, 1, D), F32),
        vm((4, 4, 1, D), F32),
        vm((4, 4, 1, D), F32),
        pltpu.SemaphoreType.DMA((17,)),
        pltpu.SemaphoreType.DMA((6,)),
        pltpu.SemaphoreType.DMA((6,)),
        pltpu.SemaphoreType.DMA((4,)),
        pltpu.SemaphoreType.DMA((4,)),
    ]
    shapes = (
        jax.ShapeDtypeStruct(fracture_pressure.shape, F32),
        jax.ShapeDtypeStruct(matrix_pressure.shape, F32),
    )
    results = pl.pallas_call(
        kernel,
        out_shape=shapes,
        in_specs=[pl.BlockSpec(memory_space=pltpu.HBM)] * 17,
        out_specs=(pl.BlockSpec(memory_space=pltpu.VMEM),) * 2,
        scratch_shapes=scratch,
        compiler_params=pltpu.CompilerParams(collective_id=0, has_side_effects=True, vmem_limit_bytes=63 << 20),
    )(*args)
    whole = pl.BlockSpec(memory_space=pltpu.VMEM)
    return pl.pallas_call(hand_over, out_shape=shapes, in_specs=[whole] * 2, out_specs=(whole,) * 2)(*results)


def solution(mesh):
    in_specs = (
        (P("gx", "gy"),) * 3
        + (P(("gx", "gy"), None, None),) * 3
        + (P(("gx", "gy")), P(("gx", "gy"), None), P(("gx", "gy")), P(("gx", "gy")), P(("gx", "gy")))
        + (P(("gx", "gy")), P(("gx", "gy")), P(("gx", "gy"), None), P(("gx", "gy")), P(("gx", "gy")), P(("gx", "gy")))
    )
    out_specs = (P(("gx", "gy"), None, None), P("gx", "gy"))
    return jax.shard_map(shards, mesh=mesh, in_specs=in_specs, out_specs=out_specs, check_vma=False)
```

```python
import jax
import jax.numpy as jnp
from jax import lax
from jax.experimental import pallas as pl
from jax.experimental.pallas import tpu as pltpu
from jax.sharding import PartitionSpec as P

LOGICAL = pl.DeviceIdType.LOGICAL
STEPS_X = (2, 1, 3, 0)
LOAD_ORDER = (13, 14, 15, 11, 12, 16, 6, 0, 7, 8, 9, 10, 3, 5, 4, 1, 2)
F32 = jnp.float32
BF16 = jnp.bfloat16
SWEEPS = 3
D = 128
QJ = 32
QI = 64


def ring(d):
    return min(d, 4 - d)


ORDER = sorted(
    [(dy, dx, dz, dc) for dy in range(4) for dx in range(4) for dz in range(4) for dc in range(2)][1:],
    key=lambda v: -(ring(v[0]) + ring(v[1]) + ring(v[2])),
)


def dot_nn(a, b):
    return lax.dot_general(a, b, (((1,), (0,)), ((), ())), preferred_element_type=F32)


def dot_nt(a, b):
    return lax.dot_general(a, b, (((1,), (1,)), ((), ())), preferred_element_type=F32)


def halves(x):
    high = x.astype(BF16).astype(F32)
    return high, (x - high).astype(BF16).astype(F32)


def spread(row, rows):
    n = row.shape[1]
    block = jnp.broadcast_to(row, (16, n)).astype(BF16)
    return jnp.broadcast_to(block[None], (rows // 16, 16, n))


def counter(rows, n):
    return (
        (lax.broadcasted_iota(jnp.int32, (rows // 16, 16, n), 0) * 16
         + lax.broadcasted_iota(jnp.int32, (rows // 16, 16, n), 1)).astype(F32).astype(BF16)
    )


def hot(row, rows):
    n = row.shape[1]
    mask = counter(rows, n) == spread(row, rows)
    return jnp.where(mask, BF16(1), BF16(0)).reshape(rows, n)


def hot_values(row, values, rows):
    n = row.shape[1]
    mask = counter(rows, n) == spread(row, rows)
    return [
        jnp.where(mask, spread(v, rows), jnp.zeros((rows // 16, 16, n), BF16)).reshape(rows, n)
        for v in values
    ]


def divide(x, by):
    whole = jnp.floor(x * (1.0 / by))
    return whole, x - whole * by


def harmonic(first, second):
    return 2.0 * first * second / (first + second)


def slots(own_ref, count, rows, q_out, lane_out, hot_own, tri):
    n = count * D

    def build(c, carry):
        at = pl.ds(pl.multiple_of(c * D, D), D)
        hot_own[:, at] = hot(own_ref[pl.ds(c, 1), :].astype(F32), D)
        return carry

    lax.fori_loop(0, count, build, 0, unroll=4)
    earlier = lax.broadcasted_iota(jnp.int32, (n, D), 0) // 256 < lax.broadcasted_iota(jnp.int32, (n, D), 1)
    base = dot_nn(hot_own[:, 0:n], jnp.where(earlier, 1.0, 0.0).astype(BF16))
    for c in range(count // 2):
        upto = dot_nn(hot_own[:, c * 256:(c + 1) * 256], tri[...])
        before = jnp.broadcast_to(base[:, c:c + 1], (D, D))
        for h in range(2):
            own = own_ref[2 * c + h:2 * c + h + 1, :]
            mask = lax.broadcasted_iota(jnp.int32, (D, D), 0) == own
            rank = jnp.sum(jnp.where(mask, upto[:, h * D:(h + 1) * D] + before, 0.0), axis=0, keepdims=True) - 1.0
            block, rest = divide(own.astype(F32), rows)
            q_out[2 * c + h:2 * c + h + 1, :] = rest
            lane_out[2 * c + h:2 * c + h + 1, :] = block * rows + rank


def pack(count, rows, values_of, planes, own_q, own_slot):
    lanes, values = [], []
    for c in range(count):
        lanes.append(hot(own_slot[c:c + 1, :], D))
        values.append(jnp.concatenate(hot_values(own_q[c:c + 1, :], values_of(c), rows), axis=0))
    out = dot_nt(jnp.concatenate(values, axis=1), jnp.concatenate(lanes, axis=1))
    return [out[p * rows:(p + 1) * rows, :] for p in range(planes)]


def columns(row, rows):
    if rows == 256:
        return hot(row, 256)
    return jnp.concatenate([hot(row, 256), hot(row - 256.0, 256)], axis=0)


def gather(table, hots, j_ref, starts, out, r_ref=None):
    for start in starts:
        js = j_ref[pl.ds(start, 8), :].astype(jnp.int32)
        rs = None if r_ref is None else r_ref[pl.ds(start, 8), :]
        for c in range(4):
            at = pl.ds(pl.multiple_of(start * D + c * 256, 256), 256)
            if r_ref is None:
                cols = hots[:, at]
            else:
                cols = jnp.concatenate([columns(rs[k:k + 1, :], table.shape[1]) for k in (2 * c, 2 * c + 1)], axis=1)
                if hots is not None:
                    hots[:, at] = cols
            got = dot_nn(table[...], cols)
            both = got[0:D, :] + got[D:2 * D, :]
            for h in range(2):
                k = 2 * c + h
                mask = lax.broadcasted_iota(jnp.int32, (D, D), 0) == js[k:k + 1, :]
                out(start + k, jnp.sum(jnp.where(mask, both[:, h * D:(h + 1) * D], 0.0), axis=0, keepdims=True))


def scatter_block(values, hots, j_ref, start, r_ref=None):
    n = values[0].shape[0]
    js = j_ref[pl.ds(start, n), :]
    at = pl.ds(pl.multiple_of(start * D, D), n * D)
    parts, made = [], []
    split = [part for v in values for part in halves(v)]
    for c in range(n):
        parts.append(jnp.concatenate(hot_values(js[c:c + 1, :], [v[c:c + 1, :] for v in split], D), axis=0))
    if r_ref is None:
        cols = hots[:, at]
    else:
        rs = r_ref[pl.ds(start, n), :]
        cols = jnp.concatenate([columns(rs[c:c + 1, :], hots.shape[0]) for c in range(n)], axis=1)
        hots[:, at] = cols
    return dot_nt(jnp.concatenate(parts, axis=1), cols)


def add_halves(total, count):
    return [total[2 * p * D:(2 * p + 1) * D, :] + total[(2 * p + 1) * D:(2 * p + 2) * D, :] for p in range(count)]


def scatter(values, hots, j_ref, chunks, r_ref=None, width=16):
    total = None
    for start in range(0, chunks, width):
        part = scatter_block([v[start:start + width, :] for v in values], hots, j_ref, start, r_ref)
        total = part if total is None else total + part
    return add_halves(total, len(values))


def set_table(tbl, q):
    high, low = halves(q)
    tbl[0:D, :] = high.astype(BF16)
    tbl[D:2 * D, :] = low.astype(BF16)


def kernel(*refs):
    given, (fnew, mnew), held = refs[0:17], refs[17:19], refs[19:36]
    (
        mp, perm, stor, fp, ia, ns,
        icell, iown, ifrac, iseg, wi,
        jfrac, jseg, jown, jffrac, jfseg, jtrans,
    ) = held
    (
        hot_own, own_slot, own_q, tri,
        near_r, near_j, near_t, served_r, served_j, isr_r, isr_j, isr_w, isr_ws, cell_r, cell_c, cell_w,
        work, rhot_srv, rhot_near, rhot_is, rhot_cells, tbl,
        q_now, cn, cs, cw, ce, inv, sto, apt, m_tot, m_wts,
        jsend, jrecv, isend, irecv, asend, arecv, rsend, rrecv, hsend, hrecv,
        load_sem, send_sem, recv_sem, hsend_sem, hrecv_sem,
    ) = refs[36:]
    gx = lax.axis_index("gx")
    gy = lax.axis_index("gy")
    me = gx * 8 + gy
    y, x, z, core = gx // 4, lax.rem(gx, 4), gy // 2, lax.rem(gy, 2)

    def peer(v):
        return (lax.rem(y + v[0], 4) * 4 + lax.rem(x + v[1], 4)) * 8 + lax.rem(z + v[2], 4) * 2 + lax.rem(core + v[3], 2)

    loads = [pltpu.make_async_copy(a, b, load_sem.at[n]) for n, (a, b) in enumerate(zip(given, held))]
    for n in LOAD_ORDER:
        loads[n].start()
    bar = pltpu.get_barrier_semaphore()
    for v in ORDER:
        pl.semaphore_signal(bar, inc=1, device_id=peer(v), device_id_type=LOGICAL)

    def ready(*numbers):
        for n in numbers:
            loads[n].wait()

    def exchange(number, src, dst, rows, steps=STEPS_X):
        for dx in steps:
            for v in ORDER:
                if v[1] == dx:
                    t = peer(v)
                    pltpu.make_async_remote_copy(
                        src.at[lax.rem(t, rows)], dst.at[me], send_sem.at[number], recv_sem.at[number, dx],
                        device_id=t, device_id_type=LOGICAL,
                    ).start()
            if dx == 0:
                pltpu.make_async_copy(src.at[lax.rem(me, rows)], dst.at[me], recv_sem.at[number, dx]).start()

    def arrived(number, dst, dx):
        part = dst.at[pl.ds(0, 32)]
        pltpu.make_async_copy(part, part, recv_sem.at[number, dx]).wait()

    def sent(number, dst):
        part = dst.at[pl.ds(0, D - 1)]
        pltpu.make_async_copy(part, part, send_sem.at[number]).wait()

    def first_row(step):
        return pl.multiple_of(lax.rem(x + step, 4) * 8, 8)

    def merge(read, rows, start=0, count=None):
        count = rows if count is None else count
        blocks = D // rows
        width = D // blocks
        lane_block = lax.broadcasted_iota(jnp.int32, (count, D), 1) // width
        out = jnp.zeros((count, D), F32)
        for k in range(blocks):
            part = pltpu.roll(read(k * rows + start, count), lax.rem((k - me // rows + blocks) * width, D), 1)
            out = jnp.where(lane_block == k, part, out)
        return out

    tri[...] = jnp.where(
        lax.broadcasted_iota(jnp.int32, (256, 256), 0) <= lax.broadcasted_iota(jnp.int32, (256, 256), 1), 1.0, 0.0
    ).astype(BF16)

    ready(13)
    slots(jown, 16, QJ, own_q, own_slot, hot_own, tri)

    def requests(c):
        high, low = divide((jffrac[c:c + 1, :] * (D * D) + jfseg[c:c + 1, :]).astype(F32), 256)
        nigh, nlow = divide((jfrac[c:c + 1, :] * (D * D) + jseg[c:c + 1, :]).astype(F32), 256)
        t_high, t_low = halves(jtrans[c:c + 1, :])
        return [high * 256.0, low, nigh * 256.0, nlow, t_high, t_low]

    ready(11, 12, 14, 15, 16)
    r_high, r_low, n_high, n_low, t_high, t_low = pack(16, QJ, requests, 6, own_q, own_slot)
    jsend[:, 0, :] = r_high + r_low
    row, col = divide(n_high + n_low, D)
    near_r[...] = row
    near_j[...] = col
    near_t[...] = t_high + t_low

    ready(0, 6, 7, 8, 9, 10)
    p_high, p_low = halves(mp[...])
    work[0:D, :] = p_high.astype(BF16)
    work[D:2 * D, :] = p_low.astype(BF16)

    row, col = divide(icell[...].astype(F32), 256)
    cell_r[0:32, :] = row
    cell_c[0:32, :] = col

    def keep_sample(c, row):
        isr_ws[c:c + 1, :] = row * wi[c:c + 1, :]

    gather(work, None, cell_r, range(0, 32, 8), keep_sample, cell_c)
    slots(iown, 32, QI, own_q, own_slot, hot_own, tri)
    pl.semaphore_wait(bar, D - 1)
    exchange(0, jsend, jrecv, QJ)

    def wells(c):
        high, low = divide((ifrac[c:c + 1, :] * (D * D) + iseg[c:c + 1, :]).astype(F32), 256)
        c_high, c_low = divide(icell[c:c + 1, :].astype(F32), 256)
        w_high, w_low = halves(wi[c:c + 1, :])
        s_high, s_low = halves(isr_ws[c:c + 1, :])
        return [high * 256.0, low, w_high, w_low, s_high, s_low, c_high, c_low]

    i_high, i_low, w_high, w_low, s_high, s_low, c_high, c_low = pack(32, QI, wells, 8, own_q, own_slot)
    isend[:, 0, 0, :] = i_high + i_low
    isend[:, 1, 0, :] = w_high + w_low
    isend[:, 2, 0, :] = s_high + s_low
    exchange(1, isend, irecv, QI)
    cell_r[...] = c_high
    cell_c[...] = c_low
    cell_w[...] = w_high + w_low

    ready(3, 4, 5)
    for f in range(4):
        at = slice(f * D, (f + 1) * D)
        p0 = fp[f].T
        effective = ns[f].T - p0
        q_now[:, at] = p0
        apt[:, at] = ia[f].T - 0.5 * effective / (0.5 + effective)
    set_table(tbl, q_now[...])

    (junc_diag,) = scatter([near_t], rhot_near, near_j, QJ, near_r)
    inv[...] = junc_diag

    def keep_answer(round_number):
        def keep(c, row):
            asend[round_number, pl.ds(c, 1), 0, :] = row

        return keep

    def answer(round_number):
        for dx in STEPS_X:
            gather(tbl, rhot_srv, served_j, [first_row(dx)], keep_answer(round_number))
            exchange(2 + round_number, asend.at[round_number], arecv.at[round_number], QJ, (dx,))

    for dx in STEPS_X:
        arrived(0, jrecv, dx)
        start = first_row(4 - dx)
        row, col = divide(merge(lambda at, n: jrecv[pl.ds(at, n), 0, :], QJ, start, 8), D)
        served_r[pl.ds(start, 8), :] = row
        served_j[pl.ds(start, 8), :] = col
        gather(tbl, rhot_srv, served_j, [start], keep_answer(0), served_r)
        exchange(2, asend.at[0], arecv.at[0], QJ, ((4 - dx) % 4,))

    for dx in STEPS_X:
        arrived(1, irecv, dx)
    row, col = divide(merge(lambda at, n: irecv[at:at + n, 0, 0, :], QI), D)
    isr_r[...] = row
    isr_j[...] = col
    isr_w[...] = merge(lambda at, n: irecv[at:at + n, 1, 0, :], QI)
    isr_ws[...] = merge(lambda at, n: irecv[at:at + n, 2, 0, :], QI)
    diag, rhs = scatter([isr_w, isr_ws], rhot_is, isr_j, QI, isr_r)
    inv[...] += diag
    sto[...] = rhs
    lane = lax.broadcasted_iota(jnp.int32, (D, D), 1)
    sub = lax.broadcasted_iota(jnp.int32, (D, D), 0)
    for f in range(4):
        at = slice(f * D, (f + 1) * D)
        ap = apt[:, at]
        cond = ap * ap * ap
        north = jnp.where(lane == 0, 0.0, harmonic(cond, pltpu.roll(cond, 1, 1)))
        south = jnp.where(lane == D - 1, 0.0, harmonic(cond, pltpu.roll(cond, D - 1, 1)))
        west = jnp.where(sub == 0, 0.0, harmonic(cond, pltpu.roll(cond, 1, 0)))
        east = jnp.where(sub == D - 1, 0.0, harmonic(cond, pltpu.roll(cond, D - 1, 0)))
        one = 1.0 / (ap + north + south + west + east + inv[:, at])
        inv[:, at] = one
        cn[:, at] = north * one
        cs[:, at] = south * one
        cw[:, at] = west * one
        ce[:, at] = east * one
        sto[:, at] = (ap * q_now[:, at] + sto[:, at]) * one

    def sweep(round_number):
        total = None
        for dx in STEPS_X:
            arrived(2 + round_number, arecv.at[round_number], dx)
            start = first_row(4 - dx)
            got = merge(lambda at, n: arecv[round_number, pl.ds(at, n), 0, :], QJ, start, 8)
            part = scatter_block([got * near_t[pl.ds(start, 8), :]], rhot_near, near_j, start)
            total = part if total is None else total + part
        (joined,) = add_halves(total, 1)
        for f in range(4):
            at = slice(f * D, (f + 1) * D)
            q = q_now[:, at]
            q_now[:, at] = (
                sto[:, at]
                + cn[:, at] * pltpu.roll(q, 1, 1)
                + cs[:, at] * pltpu.roll(q, D - 1, 1)
                + cw[:, at] * pltpu.roll(q, 1, 0)
                + ce[:, at] * pltpu.roll(q, D - 1, 0)
                + inv[:, at] * joined[:, at]
            )
        set_table(tbl, q_now[...])

    sweep(0)
    answer(1)

    ready(1, 2)
    hsend[0, 0, 0, :] = mp[0, 0:D]
    hsend[0, 1, 0, :] = mp[0, D:2 * D]
    hsend[0, 2, 0, :] = perm[0, 0:D]
    hsend[0, 3, 0, :] = perm[0, D:2 * D]
    hsend[1, 0, 0, :] = mp[D - 1, 0:D]
    hsend[1, 1, 0, :] = mp[D - 1, D:2 * D]
    hsend[1, 2, 0, :] = perm[D - 1, 0:D]
    hsend[1, 3, 0, :] = perm[D - 1, D:2 * D]
    mp_left = mp[:, 0:D].T
    mp_right = mp[:, D:2 * D].T
    perm_left = perm[:, 0:D].T
    perm_right = perm[:, D:2 * D].T
    hsend[2, 0, 0, :] = mp_left[0, :]
    hsend[2, 2, 0, :] = perm_left[0, :]
    hsend[3, 0, 0, :] = mp_right[D - 1, :]
    hsend[3, 2, 0, :] = perm_right[D - 1, :]
    hsend[2, 1, 0, :] = mp_left[0, :]
    hsend[2, 3, 0, :] = perm_left[0, :]
    hsend[3, 1, 0, :] = mp_right[D - 1, :]
    hsend[3, 3, 0, :] = perm_right[D - 1, :]
    targets = (
        lax.rem(gx + 15, 16) * 8 + gy,
        lax.rem(gx + 1, 16) * 8 + gy,
        gx * 8 + lax.rem(gy + 7, 8),
        gx * 8 + lax.rem(gy + 1, 8),
    )
    halo = [
        pltpu.make_async_remote_copy(
            hsend.at[n], hrecv.at[n], hsend_sem.at[n], hrecv_sem.at[n], device_id=t, device_id_type=LOGICAL
        )
        for n, t in enumerate(targets)
    ]
    for copy in halo:
        copy.start()
    (m_diag,) = scatter([cell_w], rhot_cells, cell_r, QI, cell_c)
    m_wts[...] = stor[...] + m_diag

    sweep(1)
    answer(2)

    for copy in halo:
        copy.wait()
    press, k = mp[...], perm[...]
    rows = lax.broadcasted_iota(jnp.int32, (D, 256), 0)
    cols = lax.broadcasted_iota(jnp.int32, (D, 256), 1)

    def wide(n, plane):
        return jnp.concatenate([hrecv[n, plane], hrecv[n, plane + 1]], axis=1)

    def tall(n, plane):
        column = jnp.broadcast_to(hrecv[n, plane], (D, D)).T
        return jnp.concatenate([column, column], axis=1)

    total = stor[...] * press
    weights = m_wts[...]
    for n, shift, axis, at_edge, outside in (
        (1, 1, 0, rows == 0, gx == 0),
        (0, D - 1, 0, rows == D - 1, gx == 15),
        (3, 1, 1, cols == 0, gy == 0),
        (2, 255, 1, cols == 255, gy == 7),
    ):
        far_p = wide(n, 0) if axis == 0 else tall(n, 0)
        far_k = wide(n, 2) if axis == 0 else tall(n, 2)
        beside_p = jnp.where(at_edge, far_p, pltpu.roll(press, shift, axis))
        beside_k = jnp.where(at_edge, far_k, pltpu.roll(k, shift, axis))
        gone = jnp.where(outside, 0.0, 1.0)
        face = harmonic(k, beside_k) * jnp.where(at_edge, gone, 1.0)
        total = total + face * beside_p
        weights = weights + face
    m_tot[...] = total
    m_wts[...] = weights

    sweep(2)

    def keep_reply(c, row):
        rsend[pl.ds(c, 1), 0, :] = row

    for dx in STEPS_X:
        start = first_row(dx)
        gather(tbl, rhot_is, isr_j, [start, pl.multiple_of(start + 32, 8)], keep_reply)
        exchange(5, rsend, rrecv, QI, (dx,))
    for f in range(4):
        fnew[f] = q_now[:, f * D:(f + 1) * D].T
    total = None
    for dx in STEPS_X:
        arrived(5, rrecv, dx)
        for more in (0, 32):
            start = pl.multiple_of(first_row(4 - dx) + more, 8)
            got = merge(lambda at, n: rrecv[pl.ds(at, n), 0, :], QI, start, 8)
            part = scatter_block([got * cell_w[pl.ds(start, 8), :]], rhot_cells, cell_r, start)
            total = part if total is None else total + part
    (m_rhs,) = add_halves(total, 1)
    mnew[...] = (m_tot[...] + m_rhs) / m_wts[...]

    sent(0, jrecv)
    sent(1, irecv)
    for n in range(SWEEPS):
        sent(2 + n, arecv.at[n])
    sent(5, rrecv)


def hand_over(a, b, a_out, b_out):
    a_out[...] = a[...]
    b_out[...] = b[...]


def shards(
    matrix_pressure, permeability, matrix_storage, fracture_pressure, initial_aperture, normal_stress,
    isect_cell, isect_owner, isect_frac, isect_seg, well_index,
    junc_frac, junc_seg, junc_owner, junc_far_frac, junc_far_seg, junc_trans,
):
    lanes = [
        a.reshape(-1, D)
        for a in (
            isect_cell, isect_owner, isect_frac, isect_seg, well_index,
            junc_frac, junc_seg, junc_owner, junc_far_frac, junc_far_seg, junc_trans,
        )
    ]
    vm = pltpu.VMEM
    args = (matrix_pressure, permeability, matrix_storage, fracture_pressure, initial_aperture, normal_stress, *lanes)
    scratch = [vm(a.shape, a.dtype) for a in args]
    scratch += [
        vm((D, 4096), BF16),
        vm((QI, D), F32),
        vm((QI, D), F32),
        vm((256, 256), BF16),
    ]
    scratch += [vm((QJ, D), F32)] * 5
    scratch += [vm((QI, D), F32)] * 7
    scratch += [
        vm((256, 256), BF16),
        vm((512, 4096), BF16),
        vm((512, 4096), BF16),
        vm((512, 8192), BF16),
        vm((256, 8192), BF16),
        vm((256, 512), BF16),
    ]
    scratch += [vm((D, 512), F32)] * 8
    scratch += [vm((D, 256), F32)] * 2
    scratch += [
        vm((QJ, 1, D), F32),
        vm((D, 1, D), F32),
        vm((QI, 3, 1, D), F32),
        vm((D, 3, 1, D), F32),
        vm((SWEEPS, QJ, 1, D), F32),
        vm((SWEEPS, D, 1, D), F32),
        vm((QI, 1, D), F32),
        vm((D, 1, D), F32),
        vm((4, 4, 1, D), F32),
        vm((4, 4, 1, D), F32),
        pltpu.SemaphoreType.DMA((17,)),
        pltpu.SemaphoreType.DMA((6,)),
        pltpu.SemaphoreType.DMA((6, 4)),
        pltpu.SemaphoreType.DMA((4,)),
        pltpu.SemaphoreType.DMA((4,)),
    ]
    shapes = (
        jax.ShapeDtypeStruct(fracture_pressure.shape, F32),
        jax.ShapeDtypeStruct(matrix_pressure.shape, F32),
    )
    results = pl.pallas_call(
        kernel,
        out_shape=shapes,
        in_specs=[pl.BlockSpec(memory_space=pltpu.HBM)] * 17,
        out_specs=(pl.BlockSpec(memory_space=pltpu.VMEM),) * 2,
        scratch_shapes=scratch,
        compiler_params=pltpu.CompilerParams(collective_id=0, has_side_effects=True, vmem_limit_bytes=63 << 20),
    )(*args)
    whole = pl.BlockSpec(memory_space=pltpu.VMEM)
    return pl.pallas_call(hand_over, out_shape=shapes, in_specs=[whole] * 2, out_specs=(whole,) * 2)(*results)


def solution(mesh):
    in_specs = (
        (P("gx", "gy"),) * 3
        + (P(("gx", "gy"), None, None),) * 3
        + (P(("gx", "gy")), P(("gx", "gy"), None), P(("gx", "gy")), P(("gx", "gy")), P(("gx", "gy")))
        + (P(("gx", "gy")), P(("gx", "gy")), P(("gx", "gy"), None), P(("gx", "gy")), P(("gx", "gy")), P(("gx", "gy")))
    )
    out_specs = (P(("gx", "gy"), None, None), P("gx", "gy"))
    return jax.shard_map(shards, mesh=mesh, in_specs=in_specs, out_specs=out_specs, check_vma=False)
```

```python
import jax
import jax.numpy as jnp
from jax import lax
from jax.experimental import pallas as pl
from jax.experimental.pallas import tpu as pltpu
from jax.sharding import PartitionSpec as P

LOGICAL = pl.DeviceIdType.LOGICAL
STEPS_X = (2, 1, 3, 0)
LOAD_ORDER = (13, 14, 15, 11, 12, 16, 6, 0, 7, 8, 9, 10, 3, 5, 4, 1, 2)
F32 = jnp.float32
BF16 = jnp.bfloat16
SWEEPS = 3
D = 128
QJ = 32
QI = 64


def ring(d):
    return min(d, 4 - d)


ORDER = sorted(
    [(dy, dx, dz, dc) for dy in range(4) for dx in range(4) for dz in range(4) for dc in range(2)][1:],
    key=lambda v: -(ring(v[0]) + ring(v[1]) + ring(v[2])),
)


def dot_nn(a, b):
    return lax.dot_general(a, b, (((1,), (0,)), ((), ())), preferred_element_type=F32)


def dot_nt(a, b):
    return lax.dot_general(a, b, (((1,), (1,)), ((), ())), preferred_element_type=F32)


def halves(x):
    high = x.astype(BF16).astype(F32)
    return high, (x - high).astype(BF16).astype(F32)


def spread(row, rows):
    n = row.shape[1]
    block = jnp.broadcast_to(row, (16, n)).astype(BF16)
    return jnp.broadcast_to(block[None], (rows // 16, 16, n))


def counter(rows, n):
    return (
        (lax.broadcasted_iota(jnp.int32, (rows // 16, 16, n), 0) * 16
         + lax.broadcasted_iota(jnp.int32, (rows // 16, 16, n), 1)).astype(F32).astype(BF16)
    )


def hot(row, rows):
    n = row.shape[1]
    mask = counter(rows, n) == spread(row, rows)
    return jnp.where(mask, BF16(1), BF16(0)).reshape(rows, n)


def hot_values(row, values, rows):
    n = row.shape[1]
    mask = counter(rows, n) == spread(row, rows)
    return [
        jnp.where(mask, spread(v, rows), jnp.zeros((rows // 16, 16, n), BF16)).reshape(rows, n)
        for v in values
    ]


def divide(x, by):
    whole = jnp.floor(x * (1.0 / by))
    return whole, x - whole * by


def harmonic(first, second):
    return 2.0 * first * second / (first + second)


def slots(own_ref, count, rows, q_out, lane_out, hot_own, tri):
    n = count * D

    def build(c, carry):
        at = pl.ds(pl.multiple_of(c * D, D), D)
        hot_own[:, at] = hot(own_ref[pl.ds(c, 1), :].astype(F32), D)
        return carry

    lax.fori_loop(0, count, build, 0, unroll=4)
    earlier = lax.broadcasted_iota(jnp.int32, (n, D), 0) // 256 < lax.broadcasted_iota(jnp.int32, (n, D), 1)
    base = dot_nn(hot_own[:, 0:n], jnp.where(earlier, 1.0, 0.0).astype(BF16))
    for c in range(count // 2):
        upto = dot_nn(hot_own[:, c * 256:(c + 1) * 256], tri[...])
        before = jnp.broadcast_to(base[:, c:c + 1], (D, D))
        for h in range(2):
            own = own_ref[2 * c + h:2 * c + h + 1, :]
            mask = lax.broadcasted_iota(jnp.int32, (D, D), 0) == own
            rank = jnp.sum(jnp.where(mask, upto[:, h * D:(h + 1) * D] + before, 0.0), axis=0, keepdims=True) - 1.0
            block, rest = divide(own.astype(F32), rows)
            q_out[2 * c + h:2 * c + h + 1, :] = rest
            lane_out[2 * c + h:2 * c + h + 1, :] = block * rows + rank


def pack(count, rows, values_of, planes, own_q, own_slot):
    lanes, values = [], []
    for c in range(count):
        lanes.append(hot(own_slot[c:c + 1, :], D))
        values.append(jnp.concatenate(hot_values(own_q[c:c + 1, :], values_of(c), rows), axis=0))
    out = dot_nt(jnp.concatenate(values, axis=1), jnp.concatenate(lanes, axis=1))
    return [out[p * rows:(p + 1) * rows, :] for p in range(planes)]


def columns(row, rows):
    if rows == 256:
        return hot(row, 256)
    return jnp.concatenate([hot(row, 256), hot(row - 256.0, 256)], axis=0)


def gather(table, hots, j_ref, starts, out, r_ref=None):
    for start in starts:
        js = j_ref[pl.ds(start, 8), :].astype(jnp.int32)
        rs = None if r_ref is None else r_ref[pl.ds(start, 8), :]
        for c in range(4):
            at = pl.ds(pl.multiple_of(start * D + c * 256, 256), 256)
            if r_ref is None:
                cols = hots[:, at]
            else:
                cols = jnp.concatenate([columns(rs[k:k + 1, :], table.shape[1]) for k in (2 * c, 2 * c + 1)], axis=1)
                if hots is not None:
                    hots[:, at] = cols
            got = dot_nn(table[...], cols)
            both = got[0:D, :] + got[D:2 * D, :]
            for h in range(2):
                k = 2 * c + h
                mask = lax.broadcasted_iota(jnp.int32, (D, D), 0) == js[k:k + 1, :]
                out(start + k, jnp.sum(jnp.where(mask, both[:, h * D:(h + 1) * D], 0.0), axis=0, keepdims=True))


def scatter_block(values, hots, j_ref, start, r_ref=None):
    n = values[0].shape[0]
    js = j_ref[pl.ds(start, n), :]
    at = pl.ds(pl.multiple_of(start * D, D), n * D)
    parts, made = [], []
    split = [part for v in values for part in halves(v)]
    for c in range(n):
        parts.append(jnp.concatenate(hot_values(js[c:c + 1, :], [v[c:c + 1, :] for v in split], D), axis=0))
    if r_ref is None:
        cols = hots[:, at]
    else:
        rs = r_ref[pl.ds(start, n), :]
        cols = jnp.concatenate([columns(rs[c:c + 1, :], hots.shape[0]) for c in range(n)], axis=1)
        hots[:, at] = cols
    return dot_nt(jnp.concatenate(parts, axis=1), cols)


def add_halves(total, count):
    return [total[2 * p * D:(2 * p + 1) * D, :] + total[(2 * p + 1) * D:(2 * p + 2) * D, :] for p in range(count)]


def scatter(values, hots, j_ref, chunks, r_ref=None, width=16):
    total = None
    for start in range(0, chunks, width):
        part = scatter_block([v[start:start + width, :] for v in values], hots, j_ref, start, r_ref)
        total = part if total is None else total + part
    return add_halves(total, len(values))


def set_table(tbl, q):
    high, low = halves(q)
    tbl[0:D, :] = high.astype(BF16)
    tbl[D:2 * D, :] = low.astype(BF16)


def kernel(*refs):
    given, (fnew, mnew), held = refs[0:17], refs[17:19], refs[19:36]
    (
        mp, perm, stor, fp, ia, ns,
        icell, iown, ifrac, iseg, wi,
        jfrac, jseg, jown, jffrac, jfseg, jtrans,
    ) = held
    (
        hot_own, own_slot, own_q, tri,
        near_r, near_j, near_t, served_r, served_j, isr_r, isr_j, isr_w, isr_ws, cell_r, cell_c, cell_w,
        work, rhot_srv, rhot_near, rhot_is, rhot_cells, tbl,
        q_now, cn, cs, cw, ce, inv, sto, apt, m_tot, m_wts,
        jsend, jrecv, isend, irecv, asend, arecv, rsend, rrecv, hsend, hrecv,
        load_sem, send_sem, recv_sem, hsend_sem, hrecv_sem,
    ) = refs[36:]
    gx = lax.axis_index("gx")
    gy = lax.axis_index("gy")
    me = gx * 8 + gy
    y, x, z, core = gx // 4, lax.rem(gx, 4), gy // 2, lax.rem(gy, 2)

    half = [lax.rem(y + d, 2) * 32 for d in range(2)]
    x_part = [lax.rem(x + d, 4) * 8 for d in range(4)]
    yx_part = [[lax.rem(y + e, 4) * 32 + x_part[d] for d in range(4)] for e in range(4)]
    low_part = [[lax.rem(z + d, 4) * 2 + lax.rem(core + e, 2) for e in range(2)] for d in range(4)]
    hx_part = [[half[e] + x_part[d] for d in range(4)] for e in range(2)]

    def peer(v):
        return yx_part[v[0]][v[1]] + low_part[v[2]][v[3]]

    def slot_row(v, rows):
        return (x_part[v[1]] if rows == QJ else hx_part[v[0] % 2][v[1]]) + low_part[v[2]][v[3]]

    loads = [pltpu.make_async_copy(a, b, load_sem.at[n]) for n, (a, b) in enumerate(zip(given, held))]
    for n in LOAD_ORDER:
        loads[n].start()
    bar = pltpu.get_barrier_semaphore()
    for v in ORDER:
        pl.semaphore_signal(bar, inc=1, device_id=peer(v), device_id_type=LOGICAL)

    def ready(*numbers):
        for n in numbers:
            loads[n].wait()

    def exchange(number, src, dst, rows, steps=STEPS_X):
        for dx in steps:
            for v in ORDER:
                if v[1] == dx:
                    t = peer(v)
                    pltpu.make_async_remote_copy(
                        src.at[slot_row(v, rows)], dst.at[me], send_sem.at[number], recv_sem.at[number, dx],
                        device_id=t, device_id_type=LOGICAL,
                    ).start()
            if dx == 0:
                pltpu.make_async_copy(src.at[lax.rem(me, rows)], dst.at[me], recv_sem.at[number, dx]).start()

    def arrived(number, dst, dx):
        part = dst.at[pl.ds(0, 32)]
        pltpu.make_async_copy(part, part, recv_sem.at[number, dx]).wait()

    def sent(number, dst):
        part = dst.at[pl.ds(0, D - 1)]
        pltpu.make_async_copy(part, part, send_sem.at[number]).wait()

    def first_row(step):
        return pl.multiple_of(lax.rem(x + step, 4) * 8, 8)

    def merge(read, rows, start=0, count=None):
        count = rows if count is None else count
        blocks = D // rows
        width = D // blocks
        lane_block = lax.broadcasted_iota(jnp.int32, (count, D), 1) // width
        out = jnp.zeros((count, D), F32)
        for k in range(blocks):
            part = pltpu.roll(read(k * rows + start, count), lax.rem((k - me // rows + blocks) * width, D), 1)
            out = jnp.where(lane_block == k, part, out)
        return out

    tri[...] = jnp.where(
        lax.broadcasted_iota(jnp.int32, (256, 256), 0) <= lax.broadcasted_iota(jnp.int32, (256, 256), 1), 1.0, 0.0
    ).astype(BF16)

    ready(13)
    slots(jown, 16, QJ, own_q, own_slot, hot_own, tri)

    def requests(c):
        high, low = divide((jffrac[c:c + 1, :] * (D * D) + jfseg[c:c + 1, :]).astype(F32), 256)
        nigh, nlow = divide((jfrac[c:c + 1, :] * (D * D) + jseg[c:c + 1, :]).astype(F32), 256)
        t_high, t_low = halves(jtrans[c:c + 1, :])
        return [high * 256.0, low, nigh * 256.0, nlow, t_high, t_low]

    ready(11, 12, 14, 15, 16)
    r_high, r_low, n_high, n_low, t_high, t_low = pack(16, QJ, requests, 6, own_q, own_slot)
    jsend[:, 0, :] = r_high + r_low
    row, col = divide(n_high + n_low, D)
    near_r[...] = row
    near_j[...] = col
    near_t[...] = t_high + t_low

    ready(0, 6, 7, 8, 9, 10)
    p_high, p_low = halves(mp[...])
    work[0:D, :] = p_high.astype(BF16)
    work[D:2 * D, :] = p_low.astype(BF16)

    row, col = divide(icell[...].astype(F32), 256)
    cell_r[0:32, :] = row
    cell_c[0:32, :] = col

    def keep_sample(c, row):
        isr_ws[c:c + 1, :] = row * wi[c:c + 1, :]

    gather(work, None, cell_r, range(0, 32, 8), keep_sample, cell_c)
    slots(iown, 32, QI, own_q, own_slot, hot_own, tri)
    (junc_diag,) = scatter([near_t], rhot_near, near_j, QJ, near_r)
    inv[...] = junc_diag
    pl.semaphore_wait(bar, D - 1)
    exchange(0, jsend, jrecv, QJ)

    def wells(c):
        high, low = divide((ifrac[c:c + 1, :] * (D * D) + iseg[c:c + 1, :]).astype(F32), 256)
        c_high, c_low = divide(icell[c:c + 1, :].astype(F32), 256)
        w_high, w_low = halves(wi[c:c + 1, :])
        s_high, s_low = halves(isr_ws[c:c + 1, :])
        return [high * 256.0, low, w_high, w_low, s_high, s_low, c_high, c_low]

    i_high, i_low, w_high, w_low, s_high, s_low, c_high, c_low = pack(32, QI, wells, 8, own_q, own_slot)
    isend[:, 0, 0, :] = i_high + i_low
    isend[:, 1, 0, :] = w_high + w_low
    isend[:, 2, 0, :] = s_high + s_low
    exchange(1, isend, irecv, QI)
    cell_r[...] = c_high
    cell_c[...] = c_low
    cell_w[...] = w_high + w_low

    ready(3, 4, 5)
    for f in range(4):
        at = slice(f * D, (f + 1) * D)
        p0 = fp[f].T
        effective = ns[f].T - p0
        q_now[:, at] = p0
        apt[:, at] = ia[f].T - 0.5 * effective / (0.5 + effective)
    set_table(tbl, q_now[...])


    def keep_answer(round_number):
        def keep(c, row):
            asend[round_number, pl.ds(c, 1), 0, :] = row

        return keep

    def answer(round_number):
        for dx in STEPS_X:
            gather(tbl, rhot_srv, served_j, [first_row(dx)], keep_answer(round_number))
            exchange(2 + round_number, asend.at[round_number], arecv.at[round_number], QJ, (dx,))

    for dx in STEPS_X:
        arrived(0, jrecv, dx)
        start = first_row(4 - dx)
        row, col = divide(merge(lambda at, n: jrecv[pl.ds(at, n), 0, :], QJ, start, 8), D)
        served_r[pl.ds(start, 8), :] = row
        served_j[pl.ds(start, 8), :] = col
        gather(tbl, rhot_srv, served_j, [start], keep_answer(0), served_r)
        exchange(2, asend.at[0], arecv.at[0], QJ, ((4 - dx) % 4,))

    for dx in STEPS_X:
        arrived(1, irecv, dx)
    row, col = divide(merge(lambda at, n: irecv[at:at + n, 0, 0, :], QI), D)
    isr_r[...] = row
    isr_j[...] = col
    isr_w[...] = merge(lambda at, n: irecv[at:at + n, 1, 0, :], QI)
    isr_ws[...] = merge(lambda at, n: irecv[at:at + n, 2, 0, :], QI)
    diag, rhs = scatter([isr_w, isr_ws], rhot_is, isr_j, QI, isr_r)
    inv[...] += diag
    sto[...] = rhs
    lane = lax.broadcasted_iota(jnp.int32, (D, D), 1)
    sub = lax.broadcasted_iota(jnp.int32, (D, D), 0)
    for f in range(4):
        at = slice(f * D, (f + 1) * D)
        ap = apt[:, at]
        cond = ap * ap * ap
        north = jnp.where(lane == 0, 0.0, harmonic(cond, pltpu.roll(cond, 1, 1)))
        south = jnp.where(lane == D - 1, 0.0, harmonic(cond, pltpu.roll(cond, D - 1, 1)))
        west = jnp.where(sub == 0, 0.0, harmonic(cond, pltpu.roll(cond, 1, 0)))
        east = jnp.where(sub == D - 1, 0.0, harmonic(cond, pltpu.roll(cond, D - 1, 0)))
        one = 1.0 / (ap + north + south + west + east + inv[:, at])
        inv[:, at] = one
        cn[:, at] = north * one
        cs[:, at] = south * one
        cw[:, at] = west * one
        ce[:, at] = east * one
        sto[:, at] = (ap * q_now[:, at] + sto[:, at]) * one

    def sweep(round_number):
        total = None
        for dx in STEPS_X:
            arrived(2 + round_number, arecv.at[round_number], dx)
            start = first_row(4 - dx)
            got = merge(lambda at, n: arecv[round_number, pl.ds(at, n), 0, :], QJ, start, 8)
            part = scatter_block([got * near_t[pl.ds(start, 8), :]], rhot_near, near_j, start)
            total = part if total is None else total + part
        (joined,) = add_halves(total, 1)
        for f in range(4):
            at = slice(f * D, (f + 1) * D)
            q = q_now[:, at]
            q_now[:, at] = (
                sto[:, at]
                + cn[:, at] * pltpu.roll(q, 1, 1)
                + cs[:, at] * pltpu.roll(q, D - 1, 1)
                + cw[:, at] * pltpu.roll(q, 1, 0)
                + ce[:, at] * pltpu.roll(q, D - 1, 0)
                + inv[:, at] * joined[:, at]
            )
        set_table(tbl, q_now[...])

    sweep(0)
    answer(1)

    ready(1, 2)
    hsend[0, 0, 0, :] = mp[0, 0:D]
    hsend[0, 1, 0, :] = mp[0, D:2 * D]
    hsend[0, 2, 0, :] = perm[0, 0:D]
    hsend[0, 3, 0, :] = perm[0, D:2 * D]
    hsend[1, 0, 0, :] = mp[D - 1, 0:D]
    hsend[1, 1, 0, :] = mp[D - 1, D:2 * D]
    hsend[1, 2, 0, :] = perm[D - 1, 0:D]
    hsend[1, 3, 0, :] = perm[D - 1, D:2 * D]
    mp_left = mp[:, 0:D].T
    mp_right = mp[:, D:2 * D].T
    perm_left = perm[:, 0:D].T
    perm_right = perm[:, D:2 * D].T
    hsend[2, 0, 0, :] = mp_left[0, :]
    hsend[2, 2, 0, :] = perm_left[0, :]
    hsend[3, 0, 0, :] = mp_right[D - 1, :]
    hsend[3, 2, 0, :] = perm_right[D - 1, :]
    hsend[2, 1, 0, :] = mp_left[0, :]
    hsend[2, 3, 0, :] = perm_left[0, :]
    hsend[3, 1, 0, :] = mp_right[D - 1, :]
    hsend[3, 3, 0, :] = perm_right[D - 1, :]
    targets = (
        lax.rem(gx + 15, 16) * 8 + gy,
        lax.rem(gx + 1, 16) * 8 + gy,
        gx * 8 + lax.rem(gy + 7, 8),
        gx * 8 + lax.rem(gy + 1, 8),
    )
    halo = [
        pltpu.make_async_remote_copy(
            hsend.at[n], hrecv.at[n], hsend_sem.at[n], hrecv_sem.at[n], device_id=t, device_id_type=LOGICAL
        )
        for n, t in enumerate(targets)
    ]
    for copy in halo:
        copy.start()
    (m_diag,) = scatter([cell_w], rhot_cells, cell_r, QI, cell_c)
    m_wts[...] = stor[...] + m_diag

    sweep(1)
    answer(2)

    for copy in halo:
        copy.wait()
    press, k = mp[...], perm[...]
    rows = lax.broadcasted_iota(jnp.int32, (D, 256), 0)
    cols = lax.broadcasted_iota(jnp.int32, (D, 256), 1)

    def wide(n, plane):
        return jnp.concatenate([hrecv[n, plane], hrecv[n, plane + 1]], axis=1)

    def tall(n, plane):
        column = jnp.broadcast_to(hrecv[n, plane], (D, D)).T
        return jnp.concatenate([column, column], axis=1)

    total = stor[...] * press
    weights = m_wts[...]
    for n, shift, axis, at_edge, outside in (
        (1, 1, 0, rows == 0, gx == 0),
        (0, D - 1, 0, rows == D - 1, gx == 15),
        (3, 1, 1, cols == 0, gy == 0),
        (2, 255, 1, cols == 255, gy == 7),
    ):
        far_p = wide(n, 0) if axis == 0 else tall(n, 0)
        far_k = wide(n, 2) if axis == 0 else tall(n, 2)
        beside_p = jnp.where(at_edge, far_p, pltpu.roll(press, shift, axis))
        beside_k = jnp.where(at_edge, far_k, pltpu.roll(k, shift, axis))
        gone = jnp.where(outside, 0.0, 1.0)
        face = harmonic(k, beside_k) * jnp.where(at_edge, gone, 1.0)
        total = total + face * beside_p
        weights = weights + face
    m_tot[...] = total
    m_wts[...] = weights

    sweep(2)

    def keep_reply(c, row):
        rsend[pl.ds(c, 1), 0, :] = row

    for dx in STEPS_X:
        start = first_row(dx)
        gather(tbl, rhot_is, isr_j, [start, pl.multiple_of(start + 32, 8)], keep_reply)
        exchange(5, rsend, rrecv, QI, (dx,))
    for f in range(4):
        fnew[f] = q_now[:, f * D:(f + 1) * D].T
    total = None
    for dx in STEPS_X:
        arrived(5, rrecv, dx)
        for more in (0, 32):
            start = pl.multiple_of(first_row(4 - dx) + more, 8)
            got = merge(lambda at, n: rrecv[pl.ds(at, n), 0, :], QI, start, 8)
            part = scatter_block([got * cell_w[pl.ds(start, 8), :]], rhot_cells, cell_r, start)
            total = part if total is None else total + part
    (m_rhs,) = add_halves(total, 1)
    mnew[...] = (m_tot[...] + m_rhs) / m_wts[...]

    sent(0, jrecv)
    sent(1, irecv)
    for n in range(SWEEPS):
        sent(2 + n, arecv.at[n])
    sent(5, rrecv)


def hand_over(a, b, a_out, b_out):
    a_out[...] = a[...]
    b_out[...] = b[...]


def shards(
    matrix_pressure, permeability, matrix_storage, fracture_pressure, initial_aperture, normal_stress,
    isect_cell, isect_owner, isect_frac, isect_seg, well_index,
    junc_frac, junc_seg, junc_owner, junc_far_frac, junc_far_seg, junc_trans,
):
    lanes = [
        a.reshape(-1, D)
        for a in (
            isect_cell, isect_owner, isect_frac, isect_seg, well_index,
            junc_frac, junc_seg, junc_owner, junc_far_frac, junc_far_seg, junc_trans,
        )
    ]
    vm = pltpu.VMEM
    args = (matrix_pressure, permeability, matrix_storage, fracture_pressure, initial_aperture, normal_stress, *lanes)
    scratch = [vm(a.shape, a.dtype) for a in args]
    scratch += [
        vm((D, 4096), BF16),
        vm((QI, D), F32),
        vm((QI, D), F32),
        vm((256, 256), BF16),
    ]
    scratch += [vm((QJ, D), F32)] * 5
    scratch += [vm((QI, D), F32)] * 7
    scratch += [
        vm((256, 256), BF16),
        vm((512, 4096), BF16),
        vm((512, 4096), BF16),
        vm((512, 8192), BF16),
        vm((256, 8192), BF16),
        vm((256, 512), BF16),
    ]
    scratch += [vm((D, 512), F32)] * 8
    scratch += [vm((D, 256), F32)] * 2
    scratch += [
        vm((QJ, 1, D), F32),
        vm((D, 1, D), F32),
        vm((QI, 3, 1, D), F32),
        vm((D, 3, 1, D), F32),
        vm((SWEEPS, QJ, 1, D), F32),
        vm((SWEEPS, D, 1, D), F32),
        vm((QI, 1, D), F32),
        vm((D, 1, D), F32),
        vm((4, 4, 1, D), F32),
        vm((4, 4, 1, D), F32),
        pltpu.SemaphoreType.DMA((17,)),
        pltpu.SemaphoreType.DMA((6,)),
        pltpu.SemaphoreType.DMA((6, 4)),
        pltpu.SemaphoreType.DMA((4,)),
        pltpu.SemaphoreType.DMA((4,)),
    ]
    shapes = (
        jax.ShapeDtypeStruct(fracture_pressure.shape, F32),
        jax.ShapeDtypeStruct(matrix_pressure.shape, F32),
    )
    results = pl.pallas_call(
        kernel,
        out_shape=shapes,
        in_specs=[pl.BlockSpec(memory_space=pltpu.HBM)] * 17,
        out_specs=(pl.BlockSpec(memory_space=pltpu.VMEM),) * 2,
        scratch_shapes=scratch,
        compiler_params=pltpu.CompilerParams(collective_id=0, has_side_effects=True, vmem_limit_bytes=63 << 20),
    )(*args)
    whole = pl.BlockSpec(memory_space=pltpu.VMEM)
    return pl.pallas_call(hand_over, out_shape=shapes, in_specs=[whole] * 2, out_specs=(whole,) * 2)(*results)


def solution(mesh):
    in_specs = (
        (P("gx", "gy"),) * 3
        + (P(("gx", "gy"), None, None),) * 3
        + (P(("gx", "gy")), P(("gx", "gy"), None), P(("gx", "gy")), P(("gx", "gy")), P(("gx", "gy")))
        + (P(("gx", "gy")), P(("gx", "gy")), P(("gx", "gy"), None), P(("gx", "gy")), P(("gx", "gy")), P(("gx", "gy")))
    )
    out_specs = (P(("gx", "gy"), None, None), P("gx", "gy"))
    return jax.shard_map(shards, mesh=mesh, in_specs=in_specs, out_specs=out_specs, check_vma=False)
```
